256 devices in a mesh: section: 32 (over y, x, z_lo), tensor: 8 (over z_hi, core).
Axes of the slice: x: 4, y: 4, z: 8 (z_hi: 4, z_lo: 2; z = z_hi * 2 + z_lo), core: 2. Of those that a mesh axis runs over, the one named last changes fastest.
Arguments:
- embedded: bfloat16 [256, 4096], P(None, 'tensor'), may hold values from -6 to 6
- outbox: bfloat16 [32, 256, 4096], P('section', None, 'tensor'), may hold values from -6 to 6
- loss_grad: bfloat16 [256, 4096], P(None, 'tensor'), may hold values from -6 to 6
- grad_outbox: bfloat16 [32, 256, 4096], P('section', None, 'tensor'), may hold values from -6 to 6
- stash_held: bfloat16 [32, 256, 4096], P('section', None, 'tensor'), may hold values from -6 to 6
- norm_gain: bfloat16 [32, 4096], P('section', 'tensor'), may hold values from 0.099609375 to 1.8984375
- w_query: bfloat16 [32, 4096, 4096], P('section', None, 'tensor'), may hold values from -4 to 4
- w_keyval: bfloat16 [32, 4096, 2048], P('section', None, 'tensor'), may hold values from -1 to 1
- w_out: bfloat16 [32, 4096, 4096], P('section', 'tensor'), may hold values from -0.125 to 0.125
Outputs:
- section_out: bfloat16 [32, 256, 4096], P('section', None, 'tensor')
- evicted: bfloat16 [32, 256, 4096], P('section', None, 'tensor')
- input_grad: bfloat16 [32, 256, 4096], P('section', None, 'tensor')
The draws below stay inside these ranges and needn't reach their ends.
All inputs are finite; a program needn't handle non-finite values.
Results may differ from the reference program's by a relative error of at most 0.013.
Values may be sent and summed in bfloat16 or wider, within the bound.
A program may use at most 64 MiB of HBM per device.

```python
import jax
import jax.numpy as jnp
from jax import lax

D = 4096
HEAD = 128
HEADS_DEV = 4
SEQ = 256
QCOLS = 4096
N_SECTION = 32
N_TENSOR = 8


def keyval_helper(key):
    base = jax.random.fold_in(key, 7)
    table = jax.random.normal(base, (N_SECTION, D, 2 * HEAD * N_TENSOR), jnp.float32) * D ** (-0.5)
    return jnp.clip(table, -1.0, 1.0)


def draw_w_keyval(key, part):
    return keyval_helper(key).astype(jnp.bfloat16)


def draw_w_query(key, part):
    noise_key = jax.random.fold_in(key, 11)
    noise = jax.random.normal(noise_key, (N_SECTION, D, N_TENSOR * HEADS_DEV * HEAD), jnp.float32) * D ** (-0.5)
    values = noise
    return jnp.clip(values, -4.0, 4.0).astype(jnp.bfloat16)


def spiked(drawn, rng, source, target, shards_of, factor):
    def block_of(dim):
        return (jnp.arange(drawn.shape[dim]) // (drawn.shape[dim] // shards_of)).reshape((-1,) + (1,) * (drawn.ndim - 1 - dim))

    near = jax.random.permutation(rng, shards_of)[block_of(target)]
    other_side = (block_of(target) + shards_of // 2) % shards_of
    return jnp.where((block_of(source) == near) | (block_of(source) == other_side), factor * drawn, drawn)


def steps_of(rng, dims, cuts, smallest, largest):
    def one(position, shards_of):
        draws = jax.random.uniform(jax.random.fold_in(jax.random.fold_in(rng, 6), position), (shards_of,), jnp.float32, smallest / len(cuts), largest / len(cuts))
        return jnp.repeat(jnp.exp(draws), dims[position] // shards_of).reshape((-1,) + (1,) * (len(dims) - position - 1))

    level = one(*cuts[0])
    for cut in cuts[1:]:
        level = level * one(*cut)
    return level


def scatter_about(stream_key, dims, spread, reach, split=(), kind=jnp.bfloat16):
    values = jax.random.normal(stream_key, dims, jnp.float32) * spread
    if len(split) > 0:
        values = steps_of(stream_key, dims, split, -0.22, 0.18) * values
    return jnp.clip(values, min=-reach, max=reach).astype(kind)


def noise_with(key, shape, width, reach, shards, heavy, held_as=jnp.bfloat16):
    entries = width * jax.random.normal(key, shape, jnp.float32)
    if shards:
        entries = entries * steps_of(key, shape, shards, -0.22, 0.18)
    return jnp.clip(spiked(entries, jax.random.fold_in(key, 3), *heavy), -reach, reach).astype(held_as)


def setup_inputs(seed: int = 0) -> dict:
    splits = jax.random.split(jax.random.key(seed), 10)
    return {
        "embedded": scatter_about(splits[0], (SEQ, D), 1.0, 6.0, ((1, 8),)),
        "outbox": scatter_about(splits[1], (N_SECTION, SEQ, D), 1.0, 6.0, ((0, 32), (2, 8))),
        "loss_grad": scatter_about(splits[2], (SEQ, D), 1.0, 6.0, ((1, 8),)),
        "grad_outbox": scatter_about(splits[3], (N_SECTION, SEQ, D), 1.0, 6.0, ((0, 32), (2, 8))),
        "stash_held": scatter_about(splits[4], (N_SECTION, SEQ, D), 1.0, 6.0, ((0, 32), (2, 8))),
        "norm_gain": jnp.clip(1.0 + 0.18 * jax.random.normal(splits[5], (N_SECTION, D), jnp.float32), 0.099609375, 1.8984375).astype(jnp.bfloat16),
        "w_query": draw_w_query(jax.random.fold_in(splits[9], 71), 0),
        "w_keyval": draw_w_keyval(jax.random.fold_in(splits[9], 71), 0),
        "w_out": noise_with(splits[8], (N_SECTION, QCOLS, D), QCOLS ** -0.5, 0.125, ((0, 32), (1, 8)), (1, 2, 8, 2.0)),
    }


EPS = 1e-05

def norm_project(x, gain, w_query, w_keyval):
    xf = x.astype(jnp.float32)
    inv = lax.rsqrt(lax.optimization_barrier(jnp.mean(xf * xf, axis=-1, keepdims=True)) + EPS)
    normed = (xf * inv * gain.astype(jnp.float32)).astype(jnp.bfloat16)
    query = jnp.dot(normed, w_query, preferred_element_type=jnp.float32).astype(jnp.bfloat16)
    keyval = jnp.dot(normed, w_keyval, preferred_element_type=jnp.float32).astype(jnp.bfloat16)
    return (inv, query, keyval)

def attend(query, keyval):
    seq = query.shape[0]
    heads = query.reshape(seq, N_TENSOR, HEADS_DEV, HEAD).astype(jnp.float32)
    pairs = keyval.reshape(seq, N_TENSOR, 2, HEAD).astype(jnp.float32)
    keys = pairs[:, :, 0]
    values = pairs[:, :, 1]
    scores = jnp.einsum('sghd,tgd->ghst', heads, keys) * HEAD ** (-0.5)
    rows = lax.broadcasted_iota(jnp.int32, (seq, seq), 0)
    cols = lax.broadcasted_iota(jnp.int32, (seq, seq), 1)
    scores = jnp.where(rows >= cols, scores, -1e+30)
    top = lax.optimization_barrier(jnp.max(scores, axis=-1, keepdims=True))
    weights = jnp.exp(scores - top)
    prob = weights / lax.optimization_barrier(jnp.sum(weights, axis=-1, keepdims=True))
    prob_low = prob.astype(jnp.bfloat16)
    attn = jnp.einsum('ghst,tgd->sghd', prob_low.astype(jnp.float32), values).astype(jnp.bfloat16)
    return (prob, prob_low, heads, keys, values, attn.reshape(seq, -1))

def section_forward(x, gain, w_query, w_keyval, w_out):
    seq = x.shape[0]
    inv, query, keyval = norm_project(x, gain, w_query, w_keyval)
    attn = attend(query, keyval)[5]
    parts = jnp.einsum('sgc,gcd->gsd', attn.reshape(seq, N_TENSOR, -1).astype(jnp.float32), w_out.reshape(N_TENSOR, -1, D).astype(jnp.float32))
    parts = lax.optimization_barrier(parts.astype(jnp.bfloat16)).astype(jnp.float32)
    mixed = lax.optimization_barrier(jnp.sum(parts, axis=0))
    return (x.astype(jnp.float32) + mixed).astype(jnp.bfloat16)

def section_backward(x, grad, gain, w_query, w_keyval, w_out):
    seq = x.shape[0]
    inv, query, keyval = norm_project(x, gain, w_query, w_keyval)
    prob, prob_low, heads, keys, values, attn = attend(query, keyval)
    d_attn = jnp.dot(grad, w_out.T, preferred_element_type=jnp.float32).astype(jnp.bfloat16)
    d_heads = d_attn.reshape(seq, N_TENSOR, HEADS_DEV, HEAD).astype(jnp.float32)
    d_prob = jnp.einsum('sghd,tgd->ghst', d_heads, values)
    d_score = prob * (d_prob - lax.optimization_barrier(jnp.sum(prob * d_prob, axis=-1, keepdims=True))) * HEAD ** (-0.5)
    d_score = lax.optimization_barrier(d_score.astype(jnp.bfloat16)).astype(jnp.float32)
    d_query = jnp.einsum('ghst,tgd->sghd', d_score, keys).astype(jnp.bfloat16)
    d_key = jnp.einsum('ghst,sghd->tgd', d_score, heads).astype(jnp.bfloat16)
    d_value = jnp.einsum('ghst,sghd->tgd', prob_low.astype(jnp.float32), d_heads).astype(jnp.bfloat16)
    d_pairs = jnp.stack([d_key, d_value], axis=2)
    parts = jnp.einsum('sgc,dgc->gsd', d_query.reshape(seq, N_TENSOR, -1).astype(jnp.float32), w_query.reshape(D, N_TENSOR, -1).astype(jnp.float32))
    parts = parts + jnp.einsum('sgc,dgc->gsd', d_pairs.reshape(seq, N_TENSOR, -1).astype(jnp.float32), w_keyval.reshape(D, N_TENSOR, -1).astype(jnp.float32))
    parts = lax.optimization_barrier(parts.astype(jnp.bfloat16)).astype(jnp.float32)
    d_normed = lax.optimization_barrier(jnp.sum(parts, axis=0))
    scaled = d_normed * gain.astype(jnp.float32)
    xf = x.astype(jnp.float32)
    correction = lax.optimization_barrier(jnp.sum(scaled * xf, axis=-1, keepdims=True)) / D
    result = grad.astype(jnp.float32) + inv * scaled - xf * inv ** 3 * correction
    return result.astype(jnp.bfloat16)

def reference(embedded, outbox, loss_grad, grad_outbox, stash_held, norm_gain, w_query, w_keyval, w_out):
    inputs = jnp.concatenate([embedded[None], outbox[:-1]], axis=0)
    grads = jnp.concatenate([grad_outbox[1:], loss_grad[None]], axis=0)
    stashed = stash_held[::-1]

    def one_section(items):
        x, grad, stash, gain, wq, wkv, wo = items
        return (section_forward(x, gain, wq, wkv, wo), section_backward(stash, grad, gain, wq, wkv, wo))
    section_out, input_grad = lax.map(one_section, (inputs, grads, stashed, norm_gain, w_query, w_keyval, w_out))
    evicted = inputs[::-1]
    return (section_out, evicted, input_grad)
```

```python
import jax
import jax.numpy as jnp
from jax import lax
from jax.sharding import PartitionSpec as P

D = 4096
HEAD = 128


EPS = 1e-05


def mirrored(value, axis, last):
    return lax.ppermute(value, axis, [(source, last - source) for source in range(last + 1)])


def shifted(value, axis, steps):
    count = lax.axis_size(axis)
    first, last = (max(0, -steps), min(count, count - steps))
    return lax.ppermute(value, axis, [(source, source + steps) for source in range(first, last)])


def normalize_project(x_full, gain_full, w_query, w_keyval):
    xf = x_full.astype(jnp.float32)
    inv = lax.rsqrt(jnp.mean(xf * xf, axis=-1, keepdims=True) + EPS)
    normed = (xf * inv * gain_full.astype(jnp.float32)).astype(jnp.bfloat16)
    query = jnp.dot(normed, w_query, preferred_element_type=jnp.float32).astype(jnp.bfloat16)
    keyval = jnp.dot(normed, w_keyval, preferred_element_type=jnp.float32).astype(jnp.bfloat16)
    return (inv, query, keyval)


def attend_local(query, keyval, heads):
    seq = query.shape[0]
    split = query.reshape(seq, heads, HEAD)
    keys = keyval[:, :HEAD]
    values = keyval[:, HEAD:]
    scores = jnp.einsum("shd,td->hst", split, keys, preferred_element_type=jnp.float32) * HEAD ** (
        -0.5
    )
    rows = lax.broadcasted_iota(jnp.int32, (seq, seq), 0)
    cols = lax.broadcasted_iota(jnp.int32, (seq, seq), 1)
    scores = jnp.where(rows >= cols, scores, -1e30)
    top = jnp.max(scores, axis=-1, keepdims=True)
    weights = jnp.exp(scores - top)
    prob = weights / jnp.sum(weights, axis=-1, keepdims=True)
    prob_low = prob.astype(jnp.bfloat16)
    attn = jnp.einsum("hst,td->shd", prob_low, values, preferred_element_type=jnp.float32)
    return (
        prob,
        prob_low,
        split,
        keys,
        values,
        attn.astype(jnp.bfloat16).reshape(seq, heads * HEAD),
    )


def local(
    embedded, outbox, loss_grad, grad_outbox, stash_held, norm_gain, w_query, w_keyval, w_out
):
    sections = lax.axis_size("section")
    position = lax.axis_index("section")
    wq = w_query[0]
    wkv = w_keyval[0]
    wo = w_out[0]
    heads = wq.shape[1] // HEAD
    arrived = shifted(outbox[0], "section", 1)
    x_shard = jnp.where(position == 0, embedded, arrived)
    coming = shifted(grad_outbox[0], "section", -1)
    grad_shard = jnp.where(position == sections - 1, loss_grad, coming)
    evicted = jnp.where(
        position == sections - 1, embedded, mirrored(outbox[0], "section", sections - 2)
    )
    fetched = mirrored(stash_held[0], "section", sections - 1)
    x_full, gain_full = (
        lax.all_gather(x_shard, "tensor", axis=1, tiled=True),
        lax.all_gather(norm_gain, "tensor", axis=1, tiled=True),
    )
    inv, query, keyval = normalize_project(x_full, gain_full, wq, wkv)
    attn = attend_local(query, keyval, heads)[5]
    partial_value = jnp.dot(attn, wo, preferred_element_type=jnp.float32)
    mixed = lax.psum_scatter(
        partial_value.astype(jnp.bfloat16), "tensor", scatter_dimension=1, tiled=True
    ).astype(jnp.float32)
    section_out = (x_shard.astype(jnp.float32) + mixed).astype(jnp.bfloat16)
    stash_full, grad_full = (
        lax.all_gather(fetched, "tensor", axis=1, tiled=True),
        lax.all_gather(grad_shard, "tensor", axis=1, tiled=True),
    )
    inv_back, query_back, keyval_back = normalize_project(stash_full, gain_full, wq, wkv)
    prob, prob_low, split, keys, values, unused = attend_local(query_back, keyval_back, heads)
    seq = stash_full.shape[0]
    d_attn = lax.dot_general(
        grad_full, wo, (((1,), (1,)), ((), ())), preferred_element_type=jnp.float32
    ).astype(jnp.bfloat16)
    d_heads = d_attn.reshape(seq, heads, HEAD)
    d_prob = jnp.einsum("shd,td->hst", d_heads, values, preferred_element_type=jnp.float32)
    d_score = prob * (d_prob - jnp.sum(prob * d_prob, axis=-1, keepdims=True)) * HEAD ** (-0.5)
    d_score = d_score.astype(jnp.bfloat16)
    d_query = jnp.einsum("hst,td->shd", d_score, keys, preferred_element_type=jnp.float32)
    d_query = d_query.astype(jnp.bfloat16).reshape(seq, heads * HEAD)
    d_key = jnp.einsum("hst,shd->td", d_score, split, preferred_element_type=jnp.float32).astype(
        jnp.bfloat16
    )
    d_value = jnp.einsum(
        "hst,shd->td", prob_low, d_heads, preferred_element_type=jnp.float32
    ).astype(jnp.bfloat16)
    d_pairs = jnp.concatenate([d_key, d_value], axis=1)
    back_terms = lax.dot_general(
        d_query, wq, (((1,), (1,)), ((), ())), preferred_element_type=jnp.float32
    )
    back_terms = back_terms + lax.dot_general(
        d_pairs, wkv, (((1,), (1,)), ((), ())), preferred_element_type=jnp.float32
    )
    gain_float = gain_full.astype(jnp.float32)
    own_total = jnp.sum(
        back_terms * gain_float * stash_full.astype(jnp.float32), axis=-1, keepdims=True
    )
    total = lax.psum(own_total, "tensor")
    summed = lax.psum_scatter(
        back_terms.astype(jnp.bfloat16), "tensor", scatter_dimension=1, tiled=True
    ).astype(jnp.float32)
    scaled = summed * norm_gain.astype(jnp.float32)
    correction = total / D
    stash_float = fetched.astype(jnp.float32)
    result = (
        grad_shard.astype(jnp.float32) + inv_back * scaled - stash_float * inv_back**3 * correction
    )
    return (section_out[None], evicted[None], result.astype(jnp.bfloat16)[None])


def solution(mesh):
    return jax.shard_map(
        local,
        mesh=mesh,
        in_specs=(
            P(None, "tensor"),
            P("section", None, "tensor"),
            P(None, "tensor"),
            P("section", None, "tensor"),
            P("section", None, "tensor"),
            P("section", "tensor"),
            P("section", None, "tensor"),
            P("section", None, "tensor"),
            P("section", "tensor", None),
        ),
        out_specs=(
            P("section", None, "tensor"),
            P("section", None, "tensor"),
            P("section", None, "tensor"),
        ),
        check_vma=False,
    )
```

```python
import jax
import jax.numpy as jnp
from jax import lax
from jax.experimental import pallas as pl
from jax.experimental.pallas import tpu as pltpu
from jax.sharding import PartitionSpec as P

HEAD = 128
EPS = 1e-05
F32 = jnp.float32
BF16 = jnp.bfloat16
NT = (((1,), (1,)), ((), ()))
TN = (((0,), (0,)), ((), ()))
STASH, GRAD, FRESH = 0, 1, 2


def dot(a, b, dims=(((1,), (0,)), ((), ()))):
    return lax.dot_general(a, b, dims, preferred_element_type=F32)


def kernel(
    embedded,
    outbox,
    loss_grad,
    grad_outbox,
    stash,
    gain,
    w_query,
    w_keyval,
    w_out,
    section_out,
    evicted,
    input_grad,
    full,
    gain_raw,
    gains,
    wq,
    wkv,
    wo,
    acc_q,
    acc_kv,
    acc_g,
    inv_ref,
    query,
    keyval,
    dquery_h,
    flat,
    dpair,
    dpair_low,
    row_sums,
    sib_out,
    sib_in,
    sums,
    own,
    ring_in,
    last_in,
    result,
    weight_sem,
    local_sem,
    gain_send,
    gain_recv,
    row_send,
    row_recv,
    near_send,
    near_recv,
    far_send,
    far_recv,
    sib_send,
    sib_recv,
    evict_send,
    evict_recv,
    rs_sib_send,
    rs_sib_recv,
    rs_send,
    rs_recv,
):
    sections = lax.axis_size("section")
    tensors = lax.axis_size("tensor")
    chips = tensors // 2
    s = lax.axis_index("section")
    t = lax.axis_index("tensor")
    seq, width = outbox.shape[1], outbox.shape[2]
    half = seq // 2
    features = width * tensors
    heads = width // HEAD
    halves = [pl.ds(0, half), pl.ds(half, half)]
    parity = lax.rem(s, 2)
    chip = t // 2
    core = lax.rem(t, 2)

    def member(chip_index, core_index):
        return 2 * lax.rem(chip_index, chips) + core_index

    above = member(chip + parity, core)
    below = member(chip + parity + chips - 1, core)
    up = member(chip + 1, core)
    down = member(chip + chips - 1, core)
    sibling = member(chip, 1 - core)
    targets = [
        sections - 1 - s,
        lax.rem(s + sections - 1, sections),
        lax.rem(s + 1, sections),
    ]
    mirror = sections - 2 - s
    goes_away = (s != sections - 1) & (mirror != s)
    stays = mirror == s
    final = s == sections - 1

    pending = []

    def remote(src, dst, send, recv, section, tensor):
        return pltpu.make_async_remote_copy(
            src_ref=src,
            dst_ref=dst,
            send_sem=send,
            recv_sem=recv,
            device_id=(section, tensor),
            device_id_type=pl.DeviceIdType.MESH,
        )

    def launch(*args):
        copy = remote(*args)
        copy.start()
        pending.append(copy)

    def arrived(ref, send, recv):
        remote(ref, ref, send, recv, s, sibling).wait_recv()

    barrier = pltpu.get_barrier_semaphore()
    peers = [(s, lax.rem(t + step, tensors)) for step in range(1, tensors)]
    peers += [(section, tensor) for section in targets for tensor in (above, below)]
    for peer in peers:
        pl.semaphore_signal(
            barrier, inc=1, device_id=peer, device_id_type=pl.DeviceIdType.MESH
        )

    @pl.when(goes_away)
    def _():
        pl.semaphore_signal(
            barrier, inc=1, device_id=(mirror, t), device_id_type=pl.DeviceIdType.MESH
        )

    gain_copy = pltpu.make_async_copy(gain, gain_raw, local_sem.at[0])
    gain_copy.start()
    weights = [
        pltpu.make_async_copy(w_query, wq, weight_sem.at[0]),
        pltpu.make_async_copy(w_keyval, wkv, weight_sem.at[1]),
    ]
    for block in range(tensors):
        weights.append(
            pltpu.make_async_copy(
                w_out.at[:, pl.ds(block * width, width)], wo.at[block], weight_sem.at[2 + block]
            )
        )
    for copy in weights:
        copy.start()
    gain_copy.wait()
    gains[t] = gain_raw[...].astype(F32)

    @pl.when(goes_away)
    def _():
        pl.semaphore_wait(barrier, len(peers) + 1)

    @pl.when(jnp.logical_not(goes_away))
    def _():
        pl.semaphore_wait(barrier, len(peers))

    def near(which, src):
        copies = []
        for part, rows in enumerate(halves):
            for side, tensor in enumerate((above, below)):
                copies.append(
                    remote(
                        src.at[rows],
                        full.at[which, t, rows],
                        near_send.at[which, side, part],
                        near_recv.at[which, side, part],
                        targets[which],
                        tensor,
                    )
                )
        return copies

    def near_start(which, usual, other, use_other):
        if other is None:
            for copy in near(which, usual):
                copy.start()
        else:

            @pl.when(use_other)
            def _():
                for copy in near(which, other):
                    copy.start()

            @pl.when(jnp.logical_not(use_other))
            def _():
                for copy in near(which, usual):
                    copy.start()

        pending.extend(near(which, usual))

    low = lax.rem(chip + parity + chips - 1, chips)
    high = lax.rem(chip + parity, chips)
    slots = [low, high, lax.rem(low + chips - 1, chips), lax.rem(high + 1, chips)]

    def pass_near(which):
        for part, rows in enumerate(halves):
            for side, ahead in enumerate((up, down)):
                here = full.at[which, 2 * slots[side] + core, rows]
                arrived(here, near_send.at[which, side, part], near_recv.at[which, side, part])
                launch(
                    here,
                    here,
                    far_send.at[which, side, part],
                    far_recv.at[which, side, part],
                    s,
                    ahead,
                )
                launch(
                    here,
                    here,
                    sib_send.at[which, side, part],
                    sib_recv.at[which, side, part],
                    s,
                    sibling,
                )

    def pass_far(which):
        for part, rows in enumerate(halves):
            for side in range(2):
                here = full.at[which, 2 * slots[2 + side] + core, rows]
                arrived(here, far_send.at[which, side, part], far_recv.at[which, side, part])
                launch(
                    here,
                    here,
                    sib_send.at[which, 2 + side, part],
                    sib_recv.at[which, 2 + side, part],
                    s,
                    sibling,
                )

    def gathered(which):
        for part, rows in enumerate(halves):
            for place in range(4):
                here = full.at[which, 2 * slots[place] + 1 - core, rows]
                arrived(here, sib_send.at[which, place, part], sib_recv.at[which, place, part])

    def project(which):
        def squares(block, total):
            value = full[which, block].astype(F32)
            value = value * value
            for piece in range(width // 128):
                total = total + value[:, piece * 128 : (piece + 1) * 128]
            return total

        total = lax.fori_loop(0, tensors, squares, jnp.zeros((seq, 128), F32))
        inv = lax.rsqrt(jnp.sum(total, axis=-1, keepdims=True) / features + EPS)
        acc_q[...] = jnp.zeros_like(acc_q)
        acc_kv[...] = jnp.zeros_like(acc_kv)

        def step(block, carry):
            normed = (full[which, block].astype(F32) * inv * gains[block]).astype(BF16)
            acc_q[...] += dot(normed, wq[block])
            acc_kv[...] += dot(normed, wkv[block])
            return carry

        lax.fori_loop(0, tensors, step, 0)
        for head in range(heads):
            query[head] = acc_q[:, head * HEAD : (head + 1) * HEAD].astype(BF16)
        for side in range(2):
            keyval[side] = acc_kv[:, side * HEAD : (side + 1) * HEAD].astype(BF16)
        return inv

    def probability(head):
        scores = dot(query[head], keyval[0], NT) * HEAD ** (-0.5)
        rows = lax.broadcasted_iota(jnp.int32, (seq, seq), 0)
        cols = lax.broadcasted_iota(jnp.int32, (seq, seq), 1)
        scores = jnp.where(rows >= cols, scores, -1e30)
        top = jnp.max(scores, axis=-1, keepdims=True)
        raised = jnp.exp(scores - top)
        return raised / jnp.sum(raised, axis=-1, keepdims=True)

    def chip_at(turn):
        return lax.rem(chip + 2 + chips - turn, chips)

    def reduce_start(which, term):
        def for_sibling(turn, carry):
            sib_out[which, turn] = term(2 * chip_at(turn) + 1 - core).astype(BF16)
            remote(
                sib_out.at[which, turn],
                sib_in.at[which, turn],
                rs_sib_send.at[which, turn],
                rs_sib_recv.at[which, turn],
                s,
                sibling,
            ).start()
            return carry

        lax.fori_loop(0, chips, for_sibling, 0)
        for turn in range(chips):
            pending.append(
                remote(
                    sib_out.at[which, turn],
                    sib_in.at[which, turn],
                    rs_sib_send.at[which, turn],
                    rs_sib_recv.at[which, turn],
                    s,
                    sibling,
                )
            )
        opening = [
            (0, 0, 0, ring_in.at[which, 0], up),
            (0, 1, 1, ring_in.at[which, 1], down),
            (1, 1, 2, last_in.at[which, 0, halves[1]], up),
            (3, 0, 3, last_in.at[which, 1, halves[0]], down),
        ]

        def sends(turn):
            return [
                remote(
                    sums.at[which, at, halves[part]],
                    dst,
                    rs_send.at[which, sem],
                    rs_recv.at[which, sem],
                    s,
                    tensor,
                )
                for at, part, sem, dst, tensor in opening
                if at == turn
            ]

        def for_self(turn, carry):
            mine = term(2 * chip_at(turn) + core)
            arrived(
                sib_in.at[which, turn], rs_sib_send.at[which, turn], rs_sib_recv.at[which, turn]
            )
            total = mine + sib_in[which, turn].astype(F32)
            sums[which, turn] = total.astype(BF16)

            @pl.when(turn == 2)
            def _():
                own[which] = total

            for at in (0, 1, 3):

                @pl.when(turn == at)
                def _():
                    for copy in sends(at):
                        copy.start()

            return carry

        lax.fori_loop(0, chips, for_self, 0)
        for at in (0, 1, 3):
            pending.extend(sends(at))

    def reduce_middle(which):
        for side, (turn, part, ahead) in enumerate(((1, 0, up), (3, 1, down))):
            rows = halves[part]
            arrived(ring_in.at[which, side], rs_send.at[which, side], rs_recv.at[which, side])
            sums[which, turn, rows] = (
                sums[which, turn, rows].astype(F32) + ring_in[which, side].astype(F32)
            ).astype(BF16)
            launch(
                sums.at[which, turn, rows],
                last_in.at[which, side, rows],
                rs_send.at[which, 4 + side],
                rs_recv.at[which, 4 + side],
                s,
                ahead,
            )

    def reduce_end(which):
        arrived(last_in.at[which, 0, halves[1]], rs_send.at[which, 2], rs_recv.at[which, 2])
        arrived(last_in.at[which, 1, halves[0]], rs_send.at[which, 3], rs_recv.at[which, 3])
        arrived(last_in.at[which, 0, halves[0]], rs_send.at[which, 4], rs_recv.at[which, 4])
        arrived(last_in.at[which, 1, halves[1]], rs_send.at[which, 5], rs_recv.at[which, 5])
        return own[which] + last_in[which, 0].astype(F32) + last_in[which, 1].astype(F32)

    near_start(STASH, stash.at[0], None, None)
    for step in range(1, tensors):
        launch(
            gains.at[t],
            gains.at[t],
            gain_send.at[step],
            gain_recv.at[step],
            s,
            lax.rem(t + step, tensors),
        )
    near_start(GRAD, grad_outbox.at[0], loss_grad, s == 0)

    evict_copy = remote(outbox.at[0], evicted.at[0], evict_send, evict_recv, mirror, t)

    @pl.when(goes_away)
    def _():
        evict_copy.start()

    @pl.when(stays)
    def _():
        pltpu.make_async_copy(outbox.at[0], evicted.at[0], local_sem.at[1]).start()

    @pl.when(final)
    def _():
        pltpu.make_async_copy(embedded, evicted.at[0], local_sem.at[1]).start()

    pass_near(STASH)
    near_start(FRESH, outbox.at[0], embedded, final)
    pass_far(STASH)
    pass_near(GRAD)
    for step in range(1, tensors):
        here = gains.at[lax.rem(t + tensors - step, tensors)]
        arrived(here, gain_send.at[step], gain_recv.at[step])
    for copy in weights:
        copy.wait()
    gathered(STASH)
    inv_back = project(STASH)
    inv_ref[...] = jnp.broadcast_to(inv_back, inv_ref.shape)
    pass_far(GRAD)
    pass_near(FRESH)
    gathered(GRAD)

    acc_g[...] = jnp.zeros_like(acc_g)

    def pull_back(block, carry):
        acc_g[...] += dot(full[GRAD, block], wo[block], NT)
        return carry

    lax.fori_loop(0, tensors, pull_back, 0)
    for head in range(heads):
        dquery_h[head] = acc_g[:, head * HEAD : (head + 1) * HEAD].astype(BF16)
    dpair[...] = jnp.zeros_like(dpair)

    def head_back(head, total):
        prob = probability(head)
        d_head = dquery_h[head]
        d_prob = dot(d_head, keyval[1], NT)
        d_score = prob * (d_prob - jnp.sum(prob * d_prob, axis=-1, keepdims=True))
        d_score = (d_score * HEAD ** (-0.5)).astype(BF16)
        d_query = dot(d_score, keyval[0]).astype(BF16)
        dpair[0] += dot(d_score, query[head], TN)
        dpair[1] += dot(prob.astype(BF16), d_head, TN)
        dquery_h[head] = d_query
        return total + d_query.astype(F32) * query[head].astype(F32)

    total = lax.fori_loop(0, heads, head_back, jnp.zeros((seq, HEAD), F32))
    for head in range(heads):
        flat[:, head * HEAD : (head + 1) * HEAD] = dquery_h[head]
    for side in range(2):
        d_low = dpair[side].astype(BF16)
        dpair_low[:, side * HEAD : (side + 1) * HEAD] = d_low
        total = total + d_low.astype(F32) * keyval[side].astype(F32)
    row_sums[t] = jnp.sum(total.T, axis=0, keepdims=True)
    for step in range(1, tensors):
        launch(
            row_sums.at[t],
            row_sums.at[t],
            row_send.at[step],
            row_recv.at[step],
            s,
            lax.rem(t + step, tensors),
        )

    def back_term(block):
        return dot(flat[...], wq[block], NT) + dot(dpair_low[...], wkv[block], NT)

    reduce_start(0, back_term)
    pass_far(FRESH)
    gathered(FRESH)
    project(FRESH)
    reduce_middle(0)

    def head_forward(head, carry):
        dquery_h[head] = dot(probability(head).astype(BF16), keyval[1]).astype(BF16)
        return carry

    lax.fori_loop(0, heads, head_forward, 0)
    for head in range(heads):
        flat[:, head * HEAD : (head + 1) * HEAD] = dquery_h[head]

    def forward_term(block):
        return dot(flat[...], wo[block])

    reduce_start(1, forward_term)

    summed = reduce_end(0)
    for step in range(1, tensors):
        here = row_sums.at[lax.rem(t + tensors - step, tensors)]
        arrived(here, row_send.at[step], row_recv.at[step])
    row = row_sums[0]
    for block in range(1, tensors):
        row = row + row_sums[block]
    column = jnp.broadcast_to(row, (128, seq)).T[:, :1]
    inv = inv_ref[:, :1]
    result[0] = (
        full[GRAD, t].astype(F32)
        + inv * (summed * gains[t])
        - full[STASH, t].astype(F32) * (inv * inv * column / features)
    ).astype(BF16)
    grad_copy = pltpu.make_async_copy(result.at[0], input_grad.at[0], local_sem.at[2])
    grad_copy.start()
    reduce_middle(1)

    @pl.when(goes_away)
    def _():
        evict_copy.wait()

    @pl.when(jnp.logical_not(goes_away))
    def _():
        pltpu.make_async_copy(outbox.at[0], evicted.at[0], local_sem.at[1]).wait()

    grad_copy.wait()
    mixed = reduce_end(1)
    result[1] = (full[FRESH, t].astype(F32) + mixed).astype(BF16)
    out_copy = pltpu.make_async_copy(result.at[1], section_out.at[0], local_sem.at[3])
    out_copy.start()
    for copy in pending:
        copy.wait_send()
    out_copy.wait()


def local(
    embedded, outbox, loss_grad, grad_outbox, stash_held, norm_gain, w_query, w_keyval, w_out
):
    tensors = lax.axis_size("tensor")
    chips = tensors // 2
    _, seq, width = outbox.shape
    half = seq // 2
    heads = width // HEAD
    shard = jax.ShapeDtypeStruct(outbox.shape, BF16)
    dma = pltpu.SemaphoreType.DMA
    anywhere = pl.BlockSpec(memory_space=pl.ANY)
    return pl.pallas_call(
        kernel,
        out_shape=(shard, shard, shard),
        in_specs=[anywhere] * 9,
        out_specs=(anywhere, anywhere, anywhere),
        scratch_shapes=[
            pltpu.VMEM((3, tensors, seq, width), BF16),
            pltpu.VMEM((1, width), BF16),
            pltpu.VMEM((tensors, 1, width), F32),
            pltpu.VMEM((tensors, width, width), BF16),
            pltpu.VMEM((tensors, width, 2 * HEAD), BF16),
            pltpu.VMEM((tensors, width, width), BF16),
            pltpu.VMEM((seq, width), F32),
            pltpu.VMEM((seq, 2 * HEAD), F32),
            pltpu.VMEM((seq, width), F32),
            pltpu.VMEM((seq, 128), F32),
            pltpu.VMEM((heads, seq, HEAD), BF16),
            pltpu.VMEM((2, seq, HEAD), BF16),
            pltpu.VMEM((heads, seq, HEAD), BF16),
            pltpu.VMEM((seq, width), BF16),
            pltpu.VMEM((2, seq, HEAD), F32),
            pltpu.VMEM((seq, 2 * HEAD), BF16),
            pltpu.VMEM((tensors, 1, seq), F32),
            pltpu.VMEM((2, chips, seq, width), BF16),
            pltpu.VMEM((2, chips, seq, width), BF16),
            pltpu.VMEM((2, chips, seq, width), BF16),
            pltpu.VMEM((2, seq, width), F32),
            pltpu.VMEM((2, 2, half, width), BF16),
            pltpu.VMEM((2, 2, seq, width), BF16),
            pltpu.VMEM((2, seq, width), BF16),
            dma((2 + tensors,)),
            dma((4,)),
            dma((tensors,)),
            dma((tensors,)),
            dma((tensors,)),
            dma((tensors,)),
            dma((3, 2, 2)),
            dma((3, 2, 2)),
            dma((3, 2, 2)),
            dma((3, 2, 2)),
            dma((3, 4, 2)),
            dma((3, 4, 2)),
            dma,
            dma,
            dma((2, chips)),
            dma((2, chips)),
            dma((2, 6)),
            dma((2, 6)),
        ],
        compiler_params=pltpu.CompilerParams(
            collective_id=0, has_side_effects=True, vmem_limit_bytes=56 * 1024 * 1024
        ),
    )(
        embedded,
        outbox,
        loss_grad,
        grad_outbox,
        stash_held,
        norm_gain,
        w_query.reshape(tensors, width, width),
        w_keyval.reshape(tensors, width, 2 * HEAD),
        w_out[0],
    )


def solution(mesh):
    return jax.shard_map(
        local,
        mesh=mesh,
        in_specs=(
            P(None, "tensor"),
            P("section", None, "tensor"),
            P(None, "tensor"),
            P("section", None, "tensor"),
            P("section", None, "tensor"),
            P("section", "tensor"),
            P("section", None, "tensor"),
            P("section", None, "tensor"),
            P("section", "tensor", None),
        ),
        out_specs=(
            P("section", None, "tensor"),
            P("section", None, "tensor"),
            P("section", None, "tensor"),
        ),
        check_vma=False,
    )
```

```python
import jax
import jax.numpy as jnp
from jax import lax
from jax.experimental import pallas as pl
from jax.experimental.pallas import tpu as pltpu
from jax.sharding import PartitionSpec as P

HEAD = 128
EPS = 1e-05
F32 = jnp.float32
BF16 = jnp.bfloat16
NT = (((1,), (1,)), ((), ()))
TN = (((0,), (0,)), ((), ()))
STASH, GRAD, FRESH = 0, 1, 2
PARTS = 4


def dot(a, b, dims=(((1,), (0,)), ((), ()))):
    return lax.dot_general(a, b, dims, preferred_element_type=F32)


def kernel(
    embedded,
    outbox,
    loss_grad,
    grad_outbox,
    stash,
    gain,
    w_query,
    w_keyval,
    w_out,
    section_out,
    evicted,
    input_grad,
    full,
    gain_raw,
    gains,
    wq,
    wkv,
    wo,
    acc_q,
    acc_kv,
    acc_g,
    inv_ref,
    query,
    keyval,
    dquery_h,
    flat,
    dpair,
    dpair_low,
    row_sums,
    sib_out,
    sib_in,
    sums,
    own,
    ring_in,
    last_in,
    result,
    staged,
    weight_sem,
    local_sem,
    gain_send,
    gain_recv,
    row_send,
    row_recv,
    near_send,
    near_recv,
    far_send,
    far_recv,
    sib_send,
    sib_recv,
    evict_send,
    evict_recv,
    rs_sib_send,
    rs_sib_recv,
    rs_send,
    rs_recv,
):
    sections = lax.axis_size("section")
    tensors = lax.axis_size("tensor")
    chips = tensors // 2
    s = lax.axis_index("section")
    t = lax.axis_index("tensor")
    seq, width = outbox.shape[1], outbox.shape[2]
    half = seq // 2
    features = width * tensors
    heads = width // HEAD
    halves = [pl.ds(0, half), pl.ds(half, half)]
    quarter = seq // PARTS
    quarters = [pl.ds(part * quarter, quarter) for part in range(PARTS)]
    parity = lax.rem(s, 2)
    chip = t // 2
    core = lax.rem(t, 2)

    def member(chip_index, core_index):
        return 2 * lax.rem(chip_index, chips) + core_index

    above = member(chip + parity, core)
    below = member(chip + parity + chips - 1, core)
    up = member(chip + 1, core)
    down = member(chip + chips - 1, core)
    sibling = member(chip, 1 - core)
    targets = [
        sections - 1 - s,
        lax.rem(s + sections - 1, sections),
        lax.rem(s + 1, sections),
    ]
    mirror = sections - 2 - s
    goes_away = (s != sections - 1) & (mirror != s)
    stays = mirror == s
    final = s == sections - 1

    pending = []

    def remote(src, dst, send, recv, section, tensor):
        return pltpu.make_async_remote_copy(
            src_ref=src,
            dst_ref=dst,
            send_sem=send,
            recv_sem=recv,
            device_id=(section, tensor),
            device_id_type=pl.DeviceIdType.MESH,
        )

    def launch(*args):
        copy = remote(*args)
        copy.start()
        pending.append(copy)

    def arrived(ref, send, recv):
        remote(ref, ref, send, recv, s, sibling).wait_recv()

    barrier = pltpu.get_barrier_semaphore()
    peers = [(s, lax.rem(t + step, tensors)) for step in range(1, tensors)]
    peers += [(section, tensor) for section in targets for tensor in (above, below)]
    for peer in peers:
        pl.semaphore_signal(
            barrier, inc=1, device_id=peer, device_id_type=pl.DeviceIdType.MESH
        )

    @pl.when(goes_away)
    def _():
        pl.semaphore_signal(
            barrier, inc=1, device_id=(mirror, t), device_id_type=pl.DeviceIdType.MESH
        )

    gain_copy = pltpu.make_async_copy(gain, gain_raw, local_sem.at[0])
    gain_copy.start()
    weights = [
        pltpu.make_async_copy(w_query, wq, weight_sem.at[0]),
        pltpu.make_async_copy(w_keyval, wkv, weight_sem.at[1]),
    ]
    for block in range(tensors):
        weights.append(
            pltpu.make_async_copy(
                w_out.at[:, pl.ds(block * width, width)], wo.at[block], weight_sem.at[2 + block]
            )
        )
    for copy in weights:
        copy.start()
    gain_copy.wait()

    @pl.when(final)
    def _():
        pltpu.make_async_copy(embedded, staged, local_sem.at[1]).start()

    @pl.when(jnp.logical_not(final))
    def _():
        pltpu.make_async_copy(outbox.at[0], staged, local_sem.at[1]).start()

    gains[t] = gain_raw[...].astype(F32)

    @pl.when(goes_away)
    def _():
        pl.semaphore_wait(barrier, len(peers) + 1)

    @pl.when(jnp.logical_not(goes_away))
    def _():
        pl.semaphore_wait(barrier, len(peers))

    def near(which, src, parts):
        return [
            remote(
                src.at[quarters[part]],
                full.at[which, t, quarters[part]],
                near_send.at[which, side, part],
                near_recv.at[which, side, part],
                targets[which],
                tensor,
            )
            for part in parts
            for side, tensor in enumerate((above, below))
        ]

    def near_start(which, src):
        for copy in near(which, src, range(PARTS)):
            copy.start()

    def fresh_start():
        @pl.when(final)
        def _():
            near_start(FRESH, embedded)

        @pl.when(jnp.logical_not(final))
        def _():
            near_start(FRESH, outbox.at[0])

    def grad_start():
        @pl.when(s == 0)
        def _():
            near_start(GRAD, loss_grad)

        @pl.when(s != 0)
        def _():
            near_start(GRAD, grad_outbox.at[0])

    low = lax.rem(chip + parity + chips - 1, chips)
    high = lax.rem(chip + parity, chips)
    slots = [low, high, lax.rem(low + chips - 1, chips), lax.rem(high + 1, chips)]

    def pass_near(which, after=None):
        for part, rows in enumerate(quarters):
            for side, ahead in enumerate((up, down)):
                here = full.at[which, 2 * slots[side] + core, rows]
                arrived(here, near_send.at[which, side, part], near_recv.at[which, side, part])
                launch(
                    here,
                    here,
                    far_send.at[which, side, part],
                    far_recv.at[which, side, part],
                    s,
                    ahead,
                )
                launch(
                    here,
                    here,
                    sib_send.at[which, side, part],
                    sib_recv.at[which, side, part],
                    s,
                    sibling,
                )
            if after is not None:
                after(part)

    def pass_far(which):
        for part, rows in enumerate(quarters):
            for side in range(2):
                here = full.at[which, 2 * slots[2 + side] + core, rows]
                arrived(here, far_send.at[which, side, part], far_recv.at[which, side, part])
                launch(
                    here,
                    here,
                    sib_send.at[which, 2 + side, part],
                    sib_recv.at[which, 2 + side, part],
                    s,
                    sibling,
                )

    def gathered(which):
        for part, rows in enumerate(quarters):
            for place in range(4):
                here = full.at[which, 2 * slots[place] + 1 - core, rows]
                arrived(here, sib_send.at[which, place, part], sib_recv.at[which, place, part])

    def project(which):
        def squares(block, total):
            value = full[which, block].astype(F32)
            value = value * value
            for piece in range(width // 128):
                total = total + value[:, piece * 128 : (piece + 1) * 128]
            return total

        total = lax.fori_loop(0, tensors, squares, jnp.zeros((seq, 128), F32))
        inv = lax.rsqrt(jnp.sum(total, axis=-1, keepdims=True) / features + EPS)
        acc_q[...] = jnp.zeros_like(acc_q)
        acc_kv[...] = jnp.zeros_like(acc_kv)

        def step(block, carry):
            normed = (full[which, block].astype(F32) * inv * gains[block]).astype(BF16)
            acc_q[...] += dot(normed, wq[block])
            acc_kv[...] += dot(normed, wkv[block])
            return carry

        lax.fori_loop(0, tensors, step, 0)
        for head in range(heads):
            query[head] = acc_q[:, head * HEAD : (head + 1) * HEAD].astype(BF16)
        for side in range(2):
            keyval[side] = acc_kv[:, side * HEAD : (side + 1) * HEAD].astype(BF16)
        return inv

    def probability(head):
        scores = dot(query[head], keyval[0], NT) * HEAD ** (-0.5)
        rows = lax.broadcasted_iota(jnp.int32, (seq, seq), 0)
        cols = lax.broadcasted_iota(jnp.int32, (seq, seq), 1)
        scores = jnp.where(rows >= cols, scores, -1e30)
        top = jnp.max(scores, axis=-1, keepdims=True)
        raised = jnp.exp(scores - top)
        return raised / jnp.sum(raised, axis=-1, keepdims=True)

    def chip_at(turn):
        return lax.rem(chip + 2 + chips - turn, chips)

    def reduce_start(which, term):
        def for_sibling(turn, carry):
            sib_out[which, turn] = term(2 * chip_at(turn) + 1 - core).astype(BF16)
            remote(
                sib_out.at[which, turn],
                sib_in.at[which, turn],
                rs_sib_send.at[which, turn],
                rs_sib_recv.at[which, turn],
                s,
                sibling,
            ).start()
            return carry

        lax.fori_loop(0, chips, for_sibling, 0)
        for turn in range(chips):
            pending.append(
                remote(
                    sib_out.at[which, turn],
                    sib_in.at[which, turn],
                    rs_sib_send.at[which, turn],
                    rs_sib_recv.at[which, turn],
                    s,
                    sibling,
                )
            )
        opening = [
            (0, 0, 0, ring_in.at[which, 0], up),
            (0, 1, 1, ring_in.at[which, 1], down),
            (1, 1, 2, last_in.at[which, 0, halves[1]], up),
            (3, 0, 3, last_in.at[which, 1, halves[0]], down),
        ]

        def sends(turn):
            return [
                remote(
                    sums.at[which, at, halves[part]],
                    dst,
                    rs_send.at[which, sem],
                    rs_recv.at[which, sem],
                    s,
                    tensor,
                )
                for at, part, sem, dst, tensor in opening
                if at == turn
            ]

        def for_self(turn, carry):
            mine = term(2 * chip_at(turn) + core)
            arrived(
                sib_in.at[which, turn], rs_sib_send.at[which, turn], rs_sib_recv.at[which, turn]
            )
            total = mine + sib_in[which, turn].astype(F32)
            sums[which, turn] = total.astype(BF16)

            @pl.when(turn == 2)
            def _():
                own[which] = total

            for at in (0, 1, 3):

                @pl.when(turn == at)
                def _():
                    for copy in sends(at):
                        copy.start()

            return carry

        lax.fori_loop(0, chips, for_self, 0)
        for at in (0, 1, 3):
            pending.extend(sends(at))

    def reduce_middle(which):
        for side, (turn, part, ahead) in enumerate(((1, 0, up), (3, 1, down))):
            rows = halves[part]
            arrived(ring_in.at[which, side], rs_send.at[which, side], rs_recv.at[which, side])
            sums[which, turn, rows] = (
                sums[which, turn, rows].astype(F32) + ring_in[which, side].astype(F32)
            ).astype(BF16)
            launch(
                sums.at[which, turn, rows],
                last_in.at[which, side, rows],
                rs_send.at[which, 4 + side],
                rs_recv.at[which, 4 + side],
                s,
                ahead,
            )

    def reduce_end(which):
        arrived(last_in.at[which, 0, halves[1]], rs_send.at[which, 2], rs_recv.at[which, 2])
        arrived(last_in.at[which, 1, halves[0]], rs_send.at[which, 3], rs_recv.at[which, 3])
        arrived(last_in.at[which, 0, halves[0]], rs_send.at[which, 4], rs_recv.at[which, 4])
        arrived(last_in.at[which, 1, halves[1]], rs_send.at[which, 5], rs_recv.at[which, 5])
        return own[which] + last_in[which, 0].astype(F32) + last_in[which, 1].astype(F32)

    for copy in near(STASH, stash.at[0], (0, 1)):
        copy.start()

    @pl.when(parity == 0)
    def _():
        fresh_start()

    @pl.when(parity == 1)
    def _():
        grad_start()

    for step in range(1, tensors):
        launch(
            gains.at[t],
            gains.at[t],
            gain_send.at[step],
            gain_recv.at[step],
            s,
            lax.rem(t + step, tensors),
        )

    def more_stash(part):
        for copy in near(STASH, stash.at[0], (part,)):
            copy.wait_send()
        if part + 2 < PARTS:
            for copy in near(STASH, stash.at[0], (part + 2,)):
                copy.start()

    pass_near(STASH, more_stash)

    @pl.when(parity == 1)
    def _():
        fresh_start()

    @pl.when(parity == 0)
    def _():
        grad_start()

    pending.extend(near(GRAD, grad_outbox.at[0], range(PARTS)))
    pending.extend(near(FRESH, outbox.at[0], range(PARTS)))
    pass_far(STASH)
    pass_near(GRAD)
    pass_near(FRESH)
    for step in range(1, tensors):
        here = gains.at[lax.rem(t + tensors - step, tensors)]
        arrived(here, gain_send.at[step], gain_recv.at[step])
    for copy in weights:
        copy.wait()
    gathered(STASH)
    inv_back = project(STASH)
    inv_ref[...] = jnp.broadcast_to(inv_back, inv_ref.shape)
    pass_far(GRAD)
    gathered(GRAD)

    acc_g[...] = jnp.zeros_like(acc_g)

    def pull_back(block, carry):
        acc_g[...] += dot(full[GRAD, block], wo[block], NT)
        return carry

    lax.fori_loop(0, tensors, pull_back, 0)
    for head in range(heads):
        dquery_h[head] = acc_g[:, head * HEAD : (head + 1) * HEAD].astype(BF16)
    dpair[...] = jnp.zeros_like(dpair)

    def head_back(head, total):
        prob = probability(head)
        d_head = dquery_h[head]
        d_prob = dot(d_head, keyval[1], NT)
        d_score = prob * (d_prob - jnp.sum(prob * d_prob, axis=-1, keepdims=True))
        d_score = (d_score * HEAD ** (-0.5)).astype(BF16)
        d_query = dot(d_score, keyval[0]).astype(BF16)
        dpair[0] += dot(d_score, query[head], TN)
        dpair[1] += dot(prob.astype(BF16), d_head, TN)
        dquery_h[head] = d_query
        return total + d_query.astype(F32) * query[head].astype(F32)

    total = lax.fori_loop(0, heads, head_back, jnp.zeros((seq, HEAD), F32))
    for head in range(heads):
        flat[:, head * HEAD : (head + 1) * HEAD] = dquery_h[head]
    for side in range(2):
        d_low = dpair[side].astype(BF16)
        dpair_low[:, side * HEAD : (side + 1) * HEAD] = d_low
        total = total + d_low.astype(F32) * keyval[side].astype(F32)
    row_sums[t] = jnp.sum(total.T, axis=0, keepdims=True)
    for step in range(1, tensors):
        launch(
            row_sums.at[t],
            row_sums.at[t],
            row_send.at[step],
            row_recv.at[step],
            s,
            lax.rem(t + step, tensors),
        )

    def back_term(block):
        return dot(flat[...], wq[block], NT) + dot(dpair_low[...], wkv[block], NT)

    reduce_start(0, back_term)

    pltpu.make_async_copy(outbox.at[0], staged, local_sem.at[1]).wait()
    evict_copy = remote(staged, evicted.at[0], evict_send, evict_recv, mirror, t)
    keep_copy = pltpu.make_async_copy(staged, evicted.at[0], local_sem.at[1])

    @pl.when(goes_away)
    def _():
        evict_copy.start()

    @pl.when(jnp.logical_not(goes_away))
    def _():
        keep_copy.start()

    pass_far(FRESH)
    gathered(FRESH)
    project(FRESH)
    reduce_middle(0)

    def head_forward(head, carry):
        dquery_h[head] = dot(probability(head).astype(BF16), keyval[1]).astype(BF16)
        return carry

    lax.fori_loop(0, heads, head_forward, 0)
    for head in range(heads):
        flat[:, head * HEAD : (head + 1) * HEAD] = dquery_h[head]

    def forward_term(block):
        return dot(flat[...], wo[block])

    reduce_start(1, forward_term)

    summed = reduce_end(0)
    for step in range(1, tensors):
        here = row_sums.at[lax.rem(t + tensors - step, tensors)]
        arrived(here, row_send.at[step], row_recv.at[step])
    row = row_sums[0]
    for block in range(1, tensors):
        row = row + row_sums[block]
    column = jnp.broadcast_to(row, (128, seq)).T[:, :1]
    inv = inv_ref[:, :1]
    result[0] = (
        full[GRAD, t].astype(F32)
        + inv * (summed * gains[t])
        - full[STASH, t].astype(F32) * (inv * inv * column / features)
    ).astype(BF16)
    grad_copy = pltpu.make_async_copy(result.at[0], input_grad.at[0], local_sem.at[2])
    grad_copy.start()
    reduce_middle(1)

    @pl.when(goes_away)
    def _():
        evict_copy.wait()

    @pl.when(jnp.logical_not(goes_away))
    def _():
        keep_copy.wait()

    grad_copy.wait()
    mixed = reduce_end(1)
    result[1] = (full[FRESH, t].astype(F32) + mixed).astype(BF16)
    out_copy = pltpu.make_async_copy(result.at[1], section_out.at[0], local_sem.at[3])
    out_copy.start()
    for copy in pending:
        copy.wait_send()
    out_copy.wait()


def hand_over(a, b, c, x, y, z):
    x[...] = a[...]
    y[...] = b[...]
    z[...] = c[...]


def local(
    embedded, outbox, loss_grad, grad_outbox, stash_held, norm_gain, w_query, w_keyval, w_out
):
    tensors = lax.axis_size("tensor")
    chips = tensors // 2
    _, seq, width = outbox.shape
    half = seq // 2
    heads = width // HEAD
    shard = jax.ShapeDtypeStruct(outbox.shape, BF16)
    dma = pltpu.SemaphoreType.DMA
    anywhere = pl.BlockSpec(memory_space=pl.ANY)
    parts = pl.pallas_call(
        kernel,
        out_shape=(shard, shard, shard),
        in_specs=[anywhere] * 9,
        out_specs=(anywhere, anywhere, anywhere),
        scratch_shapes=[
            pltpu.VMEM((3, tensors, seq, width), BF16),
            pltpu.VMEM((1, width), BF16),
            pltpu.VMEM((tensors, 1, width), F32),
            pltpu.VMEM((tensors, width, width), BF16),
            pltpu.VMEM((tensors, width, 2 * HEAD), BF16),
            pltpu.VMEM((tensors, width, width), BF16),
            pltpu.VMEM((seq, width), F32),
            pltpu.VMEM((seq, 2 * HEAD), F32),
            pltpu.VMEM((seq, width), F32),
            pltpu.VMEM((seq, 128), F32),
            pltpu.VMEM((heads, seq, HEAD), BF16),
            pltpu.VMEM((2, seq, HEAD), BF16),
            pltpu.VMEM((heads, seq, HEAD), BF16),
            pltpu.VMEM((seq, width), BF16),
            pltpu.VMEM((2, seq, HEAD), F32),
            pltpu.VMEM((seq, 2 * HEAD), BF16),
            pltpu.VMEM((tensors, 1, seq), F32),
            pltpu.VMEM((2, chips, seq, width), BF16),
            pltpu.VMEM((2, chips, seq, width), BF16),
            pltpu.VMEM((2, chips, seq, width), BF16),
            pltpu.VMEM((2, seq, width), F32),
            pltpu.VMEM((2, 2, half, width), BF16),
            pltpu.VMEM((2, 2, seq, width), BF16),
            pltpu.VMEM((2, seq, width), BF16),
            pltpu.VMEM((seq, width), BF16),
            dma((2 + tensors,)),
            dma((4,)),
            dma((tensors,)),
            dma((tensors,)),
            dma((tensors,)),
            dma((tensors,)),
            dma((3, 2, PARTS)),
            dma((3, 2, PARTS)),
            dma((3, 2, PARTS)),
            dma((3, 2, PARTS)),
            dma((3, 4, PARTS)),
            dma((3, 4, PARTS)),
            dma,
            dma,
            dma((2, chips)),
            dma((2, chips)),
            dma((2, 6)),
            dma((2, 6)),
        ],
        compiler_params=pltpu.CompilerParams(
            collective_id=0, has_side_effects=True, vmem_limit_bytes=56 * 1024 * 1024
        ),
    )(
        embedded,
        outbox,
        loss_grad,
        grad_outbox,
        stash_held,
        norm_gain,
        w_query.reshape(tensors, width, width),
        w_keyval.reshape(tensors, width, 2 * HEAD),
        w_out[0],
    )
    return pl.pallas_call(
        hand_over,
        out_shape=(shard, shard, shard),
    )(*parts)


def solution(mesh):
    return jax.shard_map(
        local,
        mesh=mesh,
        in_specs=(
            P(None, "tensor"),
            P("section", None, "tensor"),
            P(None, "tensor"),
            P("section", None, "tensor"),
            P("section", None, "tensor"),
            P("section", "tensor"),
            P("section", None, "tensor"),
            P("section", None, "tensor"),
            P("section", "tensor", None),
        ),
        out_specs=(
            P("section", None, "tensor"),
            P("section", None, "tensor"),
            P("section", None, "tensor"),
        ),
        check_vma=False,
    )
```

```python
import jax
import jax.numpy as jnp
from jax import lax
from jax.experimental import pallas as pl
from jax.experimental.pallas import tpu as pltpu
from jax.sharding import PartitionSpec as P

HEAD = 128
EPS = 1e-05
F32 = jnp.float32
BF16 = jnp.bfloat16
NT = (((1,), (1,)), ((), ()))
TN = (((0,), (0,)), ((), ()))
STASH, GRAD, FRESH = 0, 1, 2
PARTS = 4


def dot(a, b, dims=(((1,), (0,)), ((), ()))):
    return lax.dot_general(a, b, dims, preferred_element_type=F32)


def kernel(
    embedded,
    outbox,
    loss_grad,
    grad_outbox,
    stash,
    gain,
    w_query,
    w_keyval,
    w_out,
    section_out,
    evicted,
    input_grad,
    full,
    gain_raw,
    gains,
    wq,
    wkv,
    wo,
    acc_q,
    acc_kv,
    acc_g,
    inv_ref,
    query,
    keyval,
    dquery_h,
    flat,
    dpair,
    dpair_low,
    row_sums,
    sib_out,
    sib_in,
    sums,
    own,
    ring_in,
    last_in,
    result,
    staged,
    probs,
    weight_sem,
    local_sem,
    gain_send,
    gain_recv,
    row_send,
    row_recv,
    near_send,
    near_recv,
    far_send,
    far_recv,
    sib_send,
    sib_recv,
    evict_send,
    evict_recv,
    rs_sib_send,
    rs_sib_recv,
    rs_send,
    rs_recv,
):
    sections = lax.axis_size("section")
    tensors = lax.axis_size("tensor")
    chips = tensors // 2
    s = lax.axis_index("section")
    t = lax.axis_index("tensor")
    seq, width = outbox.shape[1], outbox.shape[2]
    half = seq // 2
    features = width * tensors
    heads = width // HEAD
    halves = [pl.ds(0, half), pl.ds(half, half)]
    quarter = seq // PARTS
    quarters = [pl.ds(part * quarter, quarter) for part in range(PARTS)]
    parity = lax.rem(s, 2)
    chip = t // 2
    core = lax.rem(t, 2)

    def member(chip_index, core_index):
        return 2 * lax.rem(chip_index, chips) + core_index

    above = member(chip + parity, core)
    below = member(chip + parity + chips - 1, core)
    up = member(chip + 1, core)
    down = member(chip + chips - 1, core)
    sibling = member(chip, 1 - core)
    targets = [
        sections - 1 - s,
        lax.rem(s + sections - 1, sections),
        lax.rem(s + 1, sections),
    ]
    mirror = sections - 2 - s
    goes_away = (s != sections - 1) & (mirror != s)
    stays = mirror == s
    final = s == sections - 1

    pending = []

    def remote(src, dst, send, recv, section, tensor):
        return pltpu.make_async_remote_copy(
            src_ref=src,
            dst_ref=dst,
            send_sem=send,
            recv_sem=recv,
            device_id=(section, tensor),
            device_id_type=pl.DeviceIdType.MESH,
        )

    def launch(*args):
        copy = remote(*args)
        copy.start()
        pending.append(copy)

    def arrived(ref, send, recv):
        remote(ref, ref, send, recv, s, sibling).wait_recv()

    barrier = pltpu.get_barrier_semaphore()
    peers = [(s, lax.rem(t + step, tensors)) for step in range(1, tensors)]
    peers += [(section, tensor) for section in targets for tensor in (above, below)]
    for peer in peers:
        pl.semaphore_signal(
            barrier, inc=1, device_id=peer, device_id_type=pl.DeviceIdType.MESH
        )

    @pl.when(goes_away)
    def _():
        pl.semaphore_signal(
            barrier, inc=1, device_id=(mirror, t), device_id_type=pl.DeviceIdType.MESH
        )

    gain_copy = pltpu.make_async_copy(gain, gain_raw, local_sem.at[0])
    gain_copy.start()
    weights = [
        pltpu.make_async_copy(w_query, wq, weight_sem.at[0]),
        pltpu.make_async_copy(w_keyval, wkv, weight_sem.at[1]),
    ]
    for block in range(tensors):
        weights.append(
            pltpu.make_async_copy(
                w_out.at[:, pl.ds(block * width, width)], wo.at[block], weight_sem.at[2 + block]
            )
        )
    for copy in weights:
        copy.start()
    gain_copy.wait()

    @pl.when(final)
    def _():
        pltpu.make_async_copy(embedded, staged, local_sem.at[1]).start()

    @pl.when(jnp.logical_not(final))
    def _():
        pltpu.make_async_copy(outbox.at[0], staged, local_sem.at[1]).start()

    gains[t] = gain_raw[...].astype(F32)

    @pl.when(goes_away)
    def _():
        pl.semaphore_wait(barrier, len(peers) + 1)

    @pl.when(jnp.logical_not(goes_away))
    def _():
        pl.semaphore_wait(barrier, len(peers))

    def near(which, src, parts):
        return [
            remote(
                src.at[quarters[part]],
                full.at[which, t, quarters[part]],
                near_send.at[which, side, part],
                near_recv.at[which, side, part],
                targets[which],
                tensor,
            )
            for part in parts
            for side, tensor in enumerate((above, below))
        ]

    def near_start(which, src):
        for copy in near(which, src, range(PARTS)):
            copy.start()

    def fresh_start():
        @pl.when(final)
        def _():
            near_start(FRESH, embedded)

        @pl.when(jnp.logical_not(final))
        def _():
            near_start(FRESH, outbox.at[0])

    def grad_start():
        @pl.when(s == 0)
        def _():
            near_start(GRAD, loss_grad)

        @pl.when(s != 0)
        def _():
            near_start(GRAD, grad_outbox.at[0])

    low = lax.rem(chip + parity + chips - 1, chips)
    high = lax.rem(chip + parity, chips)
    slots = [low, high, lax.rem(low + chips - 1, chips), lax.rem(high + 1, chips)]

    def pass_near(which, after=None):
        for part, rows in enumerate(quarters):
            for side, ahead in enumerate((up, down)):
                here = full.at[which, 2 * slots[side] + core, rows]
                arrived(here, near_send.at[which, side, part], near_recv.at[which, side, part])
                launch(
                    here,
                    here,
                    far_send.at[which, side, part],
                    far_recv.at[which, side, part],
                    s,
                    ahead,
                )
                launch(
                    here,
                    here,
                    sib_send.at[which, side, part],
                    sib_recv.at[which, side, part],
                    s,
                    sibling,
                )
            if after is not None:
                after(part)

    def pass_far(which):
        for part, rows in enumerate(quarters):
            for side in range(2):
                here = full.at[which, 2 * slots[2 + side] + core, rows]
                arrived(here, far_send.at[which, side, part], far_recv.at[which, side, part])
                launch(
                    here,
                    here,
                    sib_send.at[which, 2 + side, part],
                    sib_recv.at[which, 2 + side, part],
                    s,
                    sibling,
                )

    def gathered(which, places=(0, 1, 2, 3)):
        for part, rows in enumerate(quarters):
            for place in places:
                here = full.at[which, 2 * slots[place] + 1 - core, rows]
                arrived(here, sib_send.at[which, place, part], sib_recv.at[which, place, part])

    def project(which):
        def squares(block, total):
            value = full[which, block].astype(F32)
            value = value * value
            for piece in range(width // 128):
                total = total + value[:, piece * 128 : (piece + 1) * 128]
            return total

        total = lax.fori_loop(0, tensors, squares, jnp.zeros((seq, 128), F32))
        inv = lax.rsqrt(jnp.sum(total, axis=-1, keepdims=True) / features + EPS)
        acc_q[...] = jnp.zeros_like(acc_q)
        acc_kv[...] = jnp.zeros_like(acc_kv)

        def step(block, carry):
            normed = (full[which, block].astype(F32) * inv * gains[block]).astype(BF16)
            acc_q[...] += dot(normed, wq[block])
            acc_kv[...] += dot(normed, wkv[block])
            return carry

        lax.fori_loop(0, tensors, step, 0)
        for head in range(heads):
            query[head] = acc_q[:, head * HEAD : (head + 1) * HEAD].astype(BF16)
        for side in range(2):
            keyval[side] = acc_kv[:, side * HEAD : (side + 1) * HEAD].astype(BF16)
        return inv

    def probability(head):
        scores = dot(query[head], keyval[0], NT) * HEAD ** (-0.5)
        rows = lax.broadcasted_iota(jnp.int32, (seq, seq), 0)
        cols = lax.broadcasted_iota(jnp.int32, (seq, seq), 1)
        scores = jnp.where(rows >= cols, scores, -1e30)
        top = jnp.max(scores, axis=-1, keepdims=True)
        raised = jnp.exp(scores - top)
        return raised / jnp.sum(raised, axis=-1, keepdims=True)

    def chip_at(turn):
        return lax.rem(chip + 2 + chips - turn, chips)

    def reduce_start(which, term):
        def to_sibling(turn):
            return remote(
                sib_out.at[which, turn],
                sib_in.at[which, turn],
                rs_sib_send.at[which, turn],
                rs_sib_recv.at[which, turn],
                s,
                sibling,
            )

        opening = [
            (0, 0, 0, ring_in.at[which, 0], up),
            (0, 1, 1, ring_in.at[which, 1], down),
            (1, 1, 2, last_in.at[which, 0, halves[1]], up),
            (3, 0, 3, last_in.at[which, 1, halves[0]], down),
        ]

        def sends(turn):
            return [
                remote(
                    sums.at[which, at, halves[part]],
                    dst,
                    rs_send.at[which, sem],
                    rs_recv.at[which, sem],
                    s,
                    tensor,
                )
                for at, part, sem, dst, tensor in opening
                if at == turn
            ]

        def step(stage, carry):
            @pl.when(stage < chips)
            def _():
                sib_out[which, stage] = term(2 * chip_at(stage) + 1 - core).astype(BF16)
                to_sibling(stage).start()

            @pl.when(stage > 0)
            def _():
                turn = stage - 1
                mine = term(2 * chip_at(turn) + core)
                arrived(
                    sib_in.at[which, turn],
                    rs_sib_send.at[which, turn],
                    rs_sib_recv.at[which, turn],
                )
                total = mine + sib_in[which, turn].astype(F32)
                sums[which, turn] = total.astype(BF16)

                @pl.when(turn == 2)
                def _():
                    own[which] = total

                for at in (0, 1, 3):

                    @pl.when(turn == at)
                    def _():
                        for copy in sends(at):
                            copy.start()

            return carry

        lax.fori_loop(0, chips + 1, step, 0)
        pending.extend(to_sibling(turn) for turn in range(chips))
        for at in (0, 1, 3):
            pending.extend(sends(at))

    def reduce_middle(which):
        for side, (turn, part, ahead) in enumerate(((1, 0, up), (3, 1, down))):
            rows = halves[part]
            arrived(ring_in.at[which, side], rs_send.at[which, side], rs_recv.at[which, side])
            sums[which, turn, rows] = (
                sums[which, turn, rows].astype(F32) + ring_in[which, side].astype(F32)
            ).astype(BF16)
            launch(
                sums.at[which, turn, rows],
                last_in.at[which, side, rows],
                rs_send.at[which, 4 + side],
                rs_recv.at[which, 4 + side],
                s,
                ahead,
            )

    def reduce_end(which):
        arrived(last_in.at[which, 0, halves[1]], rs_send.at[which, 2], rs_recv.at[which, 2])
        arrived(last_in.at[which, 1, halves[0]], rs_send.at[which, 3], rs_recv.at[which, 3])
        arrived(last_in.at[which, 0, halves[0]], rs_send.at[which, 4], rs_recv.at[which, 4])
        arrived(last_in.at[which, 1, halves[1]], rs_send.at[which, 5], rs_recv.at[which, 5])
        return own[which] + last_in[which, 0].astype(F32) + last_in[which, 1].astype(F32)

    for copy in near(STASH, stash.at[0], (0, 1)):
        copy.start()

    @pl.when(parity == 0)
    def _():
        fresh_start()

    @pl.when(parity == 1)
    def _():
        grad_start()

    for step in range(1, tensors):
        launch(
            gains.at[t],
            gains.at[t],
            gain_send.at[step],
            gain_recv.at[step],
            s,
            lax.rem(t + step, tensors),
        )

    def more_stash(part):
        for copy in near(STASH, stash.at[0], (part,)):
            copy.wait_send()
        if part + 2 < PARTS:
            for copy in near(STASH, stash.at[0], (part + 2,)):
                copy.start()

    pass_near(STASH, more_stash)

    @pl.when(parity == 1)
    def _():
        fresh_start()

    @pl.when(parity == 0)
    def _():
        grad_start()

    pending.extend(near(GRAD, grad_outbox.at[0], range(PARTS)))
    pending.extend(near(FRESH, outbox.at[0], range(PARTS)))
    pass_far(STASH)
    pass_near(GRAD)
    for step in range(1, tensors):
        here = gains.at[lax.rem(t + tensors - step, tensors)]
        arrived(here, gain_send.at[step], gain_recv.at[step])
    for copy in weights:
        copy.wait()
    gathered(STASH)
    inv_back = project(STASH)
    inv_ref[...] = jnp.broadcast_to(inv_back, inv_ref.shape)

    def keep_probability(head, carry):
        probs[head] = probability(head)
        return carry

    lax.fori_loop(0, heads, keep_probability, 0)
    acc_g[...] = jnp.zeros_like(acc_g)

    def pull_back(places):
        def step(at, carry):
            block = 2 * slots[places[0]] + at
            other = 2 * slots[places[1]] + at
            acc_g[...] += dot(full[GRAD, block], wo[block], NT) + dot(
                full[GRAD, other], wo[other], NT
            )
            return carry

        gathered(GRAD, places)
        lax.fori_loop(0, 2, step, 0)

    pull_back((0, 1))
    pass_near(FRESH)
    pass_far(GRAD)
    pull_back((2, 3))
    for head in range(heads):
        dquery_h[head] = acc_g[:, head * HEAD : (head + 1) * HEAD].astype(BF16)
    dpair[...] = jnp.zeros_like(dpair)

    def head_back(head, total):
        prob = probs[head]
        d_head = dquery_h[head]
        d_prob = dot(d_head, keyval[1], NT)
        d_score = prob * (d_prob - jnp.sum(prob * d_prob, axis=-1, keepdims=True))
        d_score = (d_score * HEAD ** (-0.5)).astype(BF16)
        d_query = dot(d_score, keyval[0]).astype(BF16)
        dpair[0] += dot(d_score, query[head], TN)
        dpair[1] += dot(prob.astype(BF16), d_head, TN)
        dquery_h[head] = d_query
        return total + d_query.astype(F32) * query[head].astype(F32)

    total = lax.fori_loop(0, heads, head_back, jnp.zeros((seq, HEAD), F32))
    for head in range(heads):
        flat[:, head * HEAD : (head + 1) * HEAD] = dquery_h[head]
    for side in range(2):
        d_low = dpair[side].astype(BF16)
        dpair_low[:, side * HEAD : (side + 1) * HEAD] = d_low
        total = total + d_low.astype(F32) * keyval[side].astype(F32)
    row_sums[t] = jnp.sum(total.T, axis=0, keepdims=True)
    for step in range(1, tensors):
        launch(
            row_sums.at[t],
            row_sums.at[t],
            row_send.at[step],
            row_recv.at[step],
            s,
            lax.rem(t + step, tensors),
        )

    def back_term(block):
        return dot(flat[...], wq[block], NT) + dot(dpair_low[...], wkv[block], NT)

    reduce_start(0, back_term)

    pltpu.make_async_copy(outbox.at[0], staged, local_sem.at[1]).wait()
    evict_copy = remote(staged, evicted.at[0], evict_send, evict_recv, mirror, t)
    keep_copy = pltpu.make_async_copy(staged, evicted.at[0], local_sem.at[1])

    @pl.when(goes_away)
    def _():
        evict_copy.start()

    @pl.when(jnp.logical_not(goes_away))
    def _():
        keep_copy.start()

    pass_far(FRESH)
    gathered(FRESH)
    project(FRESH)
    reduce_middle(0)

    def head_forward(head, carry):
        dquery_h[head] = dot(probability(head).astype(BF16), keyval[1]).astype(BF16)
        return carry

    lax.fori_loop(0, heads, head_forward, 0)
    for head in range(heads):
        flat[:, head * HEAD : (head + 1) * HEAD] = dquery_h[head]

    def forward_term(block):
        return dot(flat[...], wo[block])

    reduce_start(1, forward_term)

    summed = reduce_end(0)
    for step in range(1, tensors):
        here = row_sums.at[lax.rem(t + tensors - step, tensors)]
        arrived(here, row_send.at[step], row_recv.at[step])
    row = row_sums[0]
    for block in range(1, tensors):
        row = row + row_sums[block]
    column = jnp.broadcast_to(row, (128, seq)).T[:, :1]
    inv = inv_ref[:, :1]
    result[0] = (
        full[GRAD, t].astype(F32)
        + inv * (summed * gains[t])
        - full[STASH, t].astype(F32) * (inv * inv * column / features)
    ).astype(BF16)
    grad_copy = pltpu.make_async_copy(result.at[0], input_grad.at[0], local_sem.at[2])
    grad_copy.start()
    reduce_middle(1)

    @pl.when(goes_away)
    def _():
        evict_copy.wait()

    @pl.when(jnp.logical_not(goes_away))
    def _():
        keep_copy.wait()

    grad_copy.wait()
    mixed = reduce_end(1)
    result[1] = (full[FRESH, t].astype(F32) + mixed).astype(BF16)
    out_copy = pltpu.make_async_copy(result.at[1], section_out.at[0], local_sem.at[3])
    out_copy.start()
    for copy in pending:
        copy.wait_send()
    out_copy.wait()


def hand_over(*refs):
    sources, targets = refs[:3], refs[3:6]
    staged, sems = refs[6:]
    inward = [
        pltpu.make_async_copy(sources[at], staged.at[at], sems.at[0, at]) for at in range(3)
    ]
    outward = [
        pltpu.make_async_copy(staged.at[at], targets[at], sems.at[1, at]) for at in range(3)
    ]
    for copy in inward:
        copy.start()
    for came, goes in zip(inward, outward):
        came.wait()
        goes.start()
    for copy in outward:
        copy.wait()


def local(
    embedded, outbox, loss_grad, grad_outbox, stash_held, norm_gain, w_query, w_keyval, w_out
):
    tensors = lax.axis_size("tensor")
    chips = tensors // 2
    _, seq, width = outbox.shape
    half = seq // 2
    heads = width // HEAD
    shard = jax.ShapeDtypeStruct(outbox.shape, BF16)
    dma = pltpu.SemaphoreType.DMA
    anywhere = pl.BlockSpec(memory_space=pl.ANY)
    parts = pl.pallas_call(
        kernel,
        out_shape=(shard, shard, shard),
        in_specs=[anywhere] * 9,
        out_specs=(anywhere, anywhere, anywhere),
        scratch_shapes=[
            pltpu.VMEM((3, tensors, seq, width), BF16),
            pltpu.VMEM((1, width), BF16),
            pltpu.VMEM((tensors, 1, width), F32),
            pltpu.VMEM((tensors, width, width), BF16),
            pltpu.VMEM((tensors, width, 2 * HEAD), BF16),
            pltpu.VMEM((tensors, width, width), BF16),
            pltpu.VMEM((seq, width), F32),
            pltpu.VMEM((seq, 2 * HEAD), F32),
            pltpu.VMEM((seq, width), F32),
            pltpu.VMEM((seq, 128), F32),
            pltpu.VMEM((heads, seq, HEAD), BF16),
            pltpu.VMEM((2, seq, HEAD), BF16),
            pltpu.VMEM((heads, seq, HEAD), BF16),
            pltpu.VMEM((seq, width), BF16),
            pltpu.VMEM((2, seq, HEAD), F32),
            pltpu.VMEM((seq, 2 * HEAD), BF16),
            pltpu.VMEM((tensors, 1, seq), F32),
            pltpu.VMEM((2, chips, seq, width), BF16),
            pltpu.VMEM((2, chips, seq, width), BF16),
            pltpu.VMEM((2, chips, seq, width), BF16),
            pltpu.VMEM((2, seq, width), F32),
            pltpu.VMEM((2, 2, half, width), BF16),
            pltpu.VMEM((2, 2, seq, width), BF16),
            pltpu.VMEM((2, seq, width), BF16),
            pltpu.VMEM((seq, width), BF16),
            pltpu.VMEM((heads, seq, seq), F32),
            dma((2 + tensors,)),
            dma((4,)),
            dma((tensors,)),
            dma((tensors,)),
            dma((tensors,)),
            dma((tensors,)),
            dma((3, 2, PARTS)),
            dma((3, 2, PARTS)),
            dma((3, 2, PARTS)),
            dma((3, 2, PARTS)),
            dma((3, 4, PARTS)),
            dma((3, 4, PARTS)),
            dma,
            dma,
            dma((2, chips)),
            dma((2, chips)),
            dma((2, 6)),
            dma((2, 6)),
        ],
        compiler_params=pltpu.CompilerParams(
            collective_id=0, has_side_effects=True, vmem_limit_bytes=56 * 1024 * 1024
        ),
    )(
        embedded,
        outbox,
        loss_grad,
        grad_outbox,
        stash_held,
        norm_gain,
        w_query.reshape(tensors, width, width),
        w_keyval.reshape(tensors, width, 2 * HEAD),
        w_out[0],
    )
    return pl.pallas_call(
        hand_over,
        out_shape=(shard, shard, shard),
        in_specs=[anywhere] * 3,
        out_specs=(anywhere, anywhere, anywhere),
        scratch_shapes=[pltpu.VMEM((3,) + outbox.shape, BF16), dma((2, 3))],
    )(*parts)


def solution(mesh):
    return jax.shard_map(
        local,
        mesh=mesh,
        in_specs=(
            P(None, "tensor"),
            P("section", None, "tensor"),
            P(None, "tensor"),
            P("section", None, "tensor"),
            P("section", None, "tensor"),
            P("section", "tensor"),
            P("section", None, "tensor"),
            P("section", None, "tensor"),
            P("section", "tensor", None),
        ),
        out_specs=(
            P("section", None, "tensor"),
            P("section", None, "tensor"),
            P("section", None, "tensor"),
        ),
        check_vma=False,
    )
```

```python
import jax
import jax.numpy as jnp
from jax import lax
from jax.experimental import pallas as pl
from jax.experimental.pallas import tpu as pltpu
from jax.sharding import PartitionSpec as P

HEAD = 128
EPS = 1e-05
F32 = jnp.float32
BF16 = jnp.bfloat16
NT = (((1,), (1,)), ((), ()))
TN = (((0,), (0,)), ((), ()))
STASH, GRAD, FRESH = 0, 1, 2
PARTS = 4


def dot(a, b, dims=(((1,), (0,)), ((), ()))):
    return lax.dot_general(a, b, dims, preferred_element_type=F32)


def kernel(
    embedded,
    outbox,
    loss_grad,
    grad_outbox,
    stash,
    gain,
    w_query,
    w_keyval,
    w_out,
    section_out,
    evicted,
    input_grad,
    full,
    gain_raw,
    gains,
    wq,
    wkv,
    wo,
    acc_q,
    acc_kv,
    acc_g,
    inv_ref,
    query,
    keyval,
    dquery_h,
    flat,
    dpair,
    dpair_low,
    row_sums,
    sib_out,
    sib_in,
    sums,
    own,
    ring_in,
    last_in,
    result,
    staged,
    probs,
    weight_sem,
    local_sem,
    gain_send,
    gain_recv,
    row_send,
    row_recv,
    near_send,
    near_recv,
    far_send,
    far_recv,
    sib_send,
    sib_recv,
    evict_send,
    evict_recv,
    rs_sib_send,
    rs_sib_recv,
    rs_send,
    rs_recv,
):
    sections = lax.axis_size("section")
    tensors = lax.axis_size("tensor")
    chips = tensors // 2
    s = lax.axis_index("section")
    t = lax.axis_index("tensor")
    seq, width = outbox.shape[1], outbox.shape[2]
    half = seq // 2
    features = width * tensors
    heads = width // HEAD
    halves = [pl.ds(0, half), pl.ds(half, half)]
    quarter = seq // PARTS
    quarters = [pl.ds(part * quarter, quarter) for part in range(PARTS)]
    parity = lax.rem(s, 2)
    chip = t // 2
    core = lax.rem(t, 2)

    def member(chip_index, core_index):
        return 2 * lax.rem(chip_index, chips) + core_index

    above = member(chip + parity, core)
    below = member(chip + parity + chips - 1, core)
    up = member(chip + 1, core)
    down = member(chip + chips - 1, core)
    sibling = member(chip, 1 - core)
    targets = [
        sections - 1 - s,
        lax.rem(s + sections - 1, sections),
        lax.rem(s + 1, sections),
    ]
    mirror = sections - 2 - s
    goes_away = (s != sections - 1) & (mirror != s)
    stays = mirror == s
    final = s == sections - 1

    pending = []

    def remote(src, dst, send, recv, section, tensor):
        return pltpu.make_async_remote_copy(
            src_ref=src,
            dst_ref=dst,
            send_sem=send,
            recv_sem=recv,
            device_id=(section, tensor),
            device_id_type=pl.DeviceIdType.MESH,
        )

    def launch(*args):
        copy = remote(*args)
        copy.start()
        pending.append(copy)

    def arrived(ref, send, recv):
        remote(ref, ref, send, recv, s, sibling).wait_recv()

    barrier = pltpu.get_barrier_semaphore()
    peers = [(s, lax.rem(t + step, tensors)) for step in range(1, tensors)]
    peers += [(section, tensor) for section in targets for tensor in (above, below)]
    for peer in peers:
        pl.semaphore_signal(
            barrier, inc=1, device_id=peer, device_id_type=pl.DeviceIdType.MESH
        )

    @pl.when(goes_away)
    def _():
        pl.semaphore_signal(
            barrier, inc=1, device_id=(mirror, t), device_id_type=pl.DeviceIdType.MESH
        )

    @pl.when(goes_away)
    def _():
        pl.semaphore_wait(barrier, len(peers) + 1)

    @pl.when(jnp.logical_not(goes_away))
    def _():
        pl.semaphore_wait(barrier, len(peers))

    def near(which, src, parts):
        return [
            remote(
                src.at[quarters[part]],
                full.at[which, t, quarters[part]],
                near_send.at[which, side, part],
                near_recv.at[which, side, part],
                targets[which],
                tensor,
            )
            for part in parts
            for side, tensor in enumerate((above, below))
        ]

    def near_start(which, src):
        for copy in near(which, src, range(PARTS)):
            copy.start()

    def fresh_start():
        @pl.when(final)
        def _():
            near_start(FRESH, embedded)

        @pl.when(jnp.logical_not(final))
        def _():
            near_start(FRESH, outbox.at[0])

    def grad_start():
        @pl.when(s == 0)
        def _():
            near_start(GRAD, loss_grad)

        @pl.when(s != 0)
        def _():
            near_start(GRAD, grad_outbox.at[0])

    low = lax.rem(chip + parity + chips - 1, chips)
    high = lax.rem(chip + parity, chips)
    slots = [low, high, lax.rem(low + chips - 1, chips), lax.rem(high + 1, chips)]

    def pass_near(which, after=None, parts=range(PARTS)):
        for part in parts:
            rows = quarters[part]
            for side, ahead in enumerate((up, down)):
                here = full.at[which, 2 * slots[side] + core, rows]
                arrived(here, near_send.at[which, side, part], near_recv.at[which, side, part])
                launch(
                    here,
                    here,
                    far_send.at[which, side, part],
                    far_recv.at[which, side, part],
                    s,
                    ahead,
                )
                launch(
                    here,
                    here,
                    sib_send.at[which, side, part],
                    sib_recv.at[which, side, part],
                    s,
                    sibling,
                )
            if after is not None:
                after(part)

    def pass_far(which):
        for part, rows in enumerate(quarters):
            for side in range(2):
                here = full.at[which, 2 * slots[2 + side] + core, rows]
                arrived(here, far_send.at[which, side, part], far_recv.at[which, side, part])
                launch(
                    here,
                    here,
                    sib_send.at[which, 2 + side, part],
                    sib_recv.at[which, 2 + side, part],
                    s,
                    sibling,
                )

    def gathered(which, places=(0, 1, 2, 3)):
        for part, rows in enumerate(quarters):
            for place in places:
                here = full.at[which, 2 * slots[place] + 1 - core, rows]
                arrived(here, sib_send.at[which, place, part], sib_recv.at[which, place, part])

    def project(which):
        def squares(block, total):
            value = full[which, block].astype(F32)
            value = value * value
            for piece in range(width // 128):
                total = total + value[:, piece * 128 : (piece + 1) * 128]
            return total

        total = lax.fori_loop(0, tensors, squares, jnp.zeros((seq, 128), F32))
        inv = lax.rsqrt(jnp.sum(total, axis=-1, keepdims=True) / features + EPS)
        acc_q[...] = jnp.zeros_like(acc_q)
        acc_kv[...] = jnp.zeros_like(acc_kv)

        def step(block, carry):
            normed = (full[which, block].astype(F32) * inv * gains[block]).astype(BF16)
            acc_q[...] += dot(normed, wq[block])
            acc_kv[...] += dot(normed, wkv[block])
            return carry

        lax.fori_loop(0, tensors, step, 0)
        for head in range(heads):
            query[head] = acc_q[:, head * HEAD : (head + 1) * HEAD].astype(BF16)
        for side in range(2):
            keyval[side] = acc_kv[:, side * HEAD : (side + 1) * HEAD].astype(BF16)
        return inv

    def probability(head):
        scores = dot(query[head], keyval[0], NT) * HEAD ** (-0.5)
        rows = lax.broadcasted_iota(jnp.int32, (seq, seq), 0)
        cols = lax.broadcasted_iota(jnp.int32, (seq, seq), 1)
        scores = jnp.where(rows >= cols, scores, -1e30)
        top = jnp.max(scores, axis=-1, keepdims=True)
        raised = jnp.exp(scores - top)
        return raised / jnp.sum(raised, axis=-1, keepdims=True)

    def chip_at(turn):
        return lax.rem(chip + 2 + chips - turn, chips)

    def reduce_start(which, term):
        def to_sibling(turn):
            return remote(
                sib_out.at[which, turn],
                sib_in.at[which, turn],
                rs_sib_send.at[which, turn],
                rs_sib_recv.at[which, turn],
                s,
                sibling,
            )

        opening = [
            (0, 0, 0, ring_in.at[which, 0], up),
            (0, 1, 1, ring_in.at[which, 1], down),
            (1, 1, 2, last_in.at[which, 0, halves[1]], up),
            (3, 0, 3, last_in.at[which, 1, halves[0]], down),
        ]

        def sends(turn):
            return [
                remote(
                    sums.at[which, at, halves[part]],
                    dst,
                    rs_send.at[which, sem],
                    rs_recv.at[which, sem],
                    s,
                    tensor,
                )
                for at, part, sem, dst, tensor in opening
                if at == turn
            ]

        def step(stage, carry):
            @pl.when(stage < chips)
            def _():
                sib_out[which, stage] = term(2 * chip_at(stage) + 1 - core).astype(BF16)
                to_sibling(stage).start()

            @pl.when(stage > 0)
            def _():
                turn = stage - 1
                mine = term(2 * chip_at(turn) + core)
                arrived(
                    sib_in.at[which, turn],
                    rs_sib_send.at[which, turn],
                    rs_sib_recv.at[which, turn],
                )
                total = mine + sib_in[which, turn].astype(F32)
                sums[which, turn] = total.astype(BF16)

                @pl.when(turn == 2)
                def _():
                    own[which] = total

                for at in (0, 1, 3):

                    @pl.when(turn == at)
                    def _():
                        for copy in sends(at):
                            copy.start()

            return carry

        lax.fori_loop(0, chips + 1, step, 0)
        pending.extend(to_sibling(turn) for turn in range(chips))
        for at in (0, 1, 3):
            pending.extend(sends(at))

    def reduce_middle(which):
        for side, (turn, part, ahead) in enumerate(((1, 0, up), (3, 1, down))):
            rows = halves[part]
            arrived(ring_in.at[which, side], rs_send.at[which, side], rs_recv.at[which, side])
            sums[which, turn, rows] = (
                sums[which, turn, rows].astype(F32) + ring_in[which, side].astype(F32)
            ).astype(BF16)
            launch(
                sums.at[which, turn, rows],
                last_in.at[which, side, rows],
                rs_send.at[which, 4 + side],
                rs_recv.at[which, 4 + side],
                s,
                ahead,
            )

    def reduce_end(which):
        arrived(last_in.at[which, 0, halves[1]], rs_send.at[which, 2], rs_recv.at[which, 2])
        arrived(last_in.at[which, 1, halves[0]], rs_send.at[which, 3], rs_recv.at[which, 3])
        arrived(last_in.at[which, 0, halves[0]], rs_send.at[which, 4], rs_recv.at[which, 4])
        arrived(last_in.at[which, 1, halves[1]], rs_send.at[which, 5], rs_recv.at[which, 5])
        return last_in[which, 0].astype(F32) + last_in[which, 1].astype(F32)

    for copy in near(STASH, stash.at[0], (0, 1)):
        copy.start()

    @pl.when(parity == 0)
    def _():
        fresh_start()

    @pl.when(parity == 1)
    def _():
        grad_start()

    gain_copy = pltpu.make_async_copy(gain, gain_raw, local_sem.at[0])
    gain_copy.start()
    weights = [
        pltpu.make_async_copy(w_query, wq, weight_sem.at[0]),
        pltpu.make_async_copy(w_keyval, wkv, weight_sem.at[1]),
    ]
    for block in range(tensors):
        weights.append(
            pltpu.make_async_copy(
                w_out.at[:, pl.ds(block * width, width)], wo.at[block], weight_sem.at[2 + block]
            )
        )
    for copy in weights:
        copy.start()
    gain_copy.wait()

    @pl.when(final)
    def _():
        pltpu.make_async_copy(embedded, staged, local_sem.at[1]).start()

    @pl.when(jnp.logical_not(final))
    def _():
        pltpu.make_async_copy(outbox.at[0], staged, local_sem.at[1]).start()

    gains[t] = gain_raw[...].astype(F32)

    for step in range(1, tensors):
        launch(
            gains.at[t],
            gains.at[t],
            gain_send.at[step],
            gain_recv.at[step],
            s,
            lax.rem(t + step, tensors),
        )

    def more_stash(part):
        for copy in near(STASH, stash.at[0], (part,)):
            copy.wait_send()
        if part + 2 < PARTS:
            for copy in near(STASH, stash.at[0], (part + 2,)):
                copy.start()

    pass_near(STASH, more_stash)

    @pl.when(parity == 1)
    def _():
        fresh_start()

    @pl.when(parity == 0)
    def _():
        grad_start()

    pending.extend(near(GRAD, grad_outbox.at[0], range(PARTS)))
    pending.extend(near(FRESH, outbox.at[0], range(PARTS)))
    pass_far(STASH)
    pass_near(GRAD)
    for step in range(1, tensors):
        here = gains.at[lax.rem(t + tensors - step, tensors)]
        arrived(here, gain_send.at[step], gain_recv.at[step])
    for copy in weights:
        copy.wait()
    gathered(STASH)
    pltpu.make_async_copy(outbox.at[0], staged, local_sem.at[1]).wait()
    evict_copy = remote(staged, evicted.at[0], evict_send, evict_recv, mirror, t)
    keep_copy = pltpu.make_async_copy(staged, evicted.at[0], local_sem.at[1])

    @pl.when(goes_away)
    def _():
        evict_copy.start()

    @pl.when(jnp.logical_not(goes_away))
    def _():
        keep_copy.start()

    inv_back = project(STASH)
    inv_ref[...] = jnp.broadcast_to(inv_back, inv_ref.shape)

    def keep_probability(head, carry):
        probs[head] = probability(head)
        return carry

    lax.fori_loop(0, heads, keep_probability, 0)
    acc_g[...] = jnp.zeros_like(acc_g)

    def pull_back(places):
        def step(at, carry):
            block = 2 * slots[places[0]] + at
            other = 2 * slots[places[1]] + at
            acc_g[...] += dot(full[GRAD, block], wo[block], NT) + dot(
                full[GRAD, other], wo[other], NT
            )
            return carry

        gathered(GRAD, places)
        lax.fori_loop(0, 2, step, 0)

    pull_back((0, 1))
    pass_near(FRESH, parts=(0, 1))
    pass_far(GRAD)
    pass_near(FRESH, parts=(2, 3))
    pull_back((2, 3))
    for head in range(heads):
        dquery_h[head] = acc_g[:, head * HEAD : (head + 1) * HEAD].astype(BF16)
    dpair[...] = jnp.zeros_like(dpair)

    def head_back(head, total):
        prob = probs[head]
        d_head = dquery_h[head]
        d_prob = dot(d_head, keyval[1], NT)
        d_score = prob * (d_prob - jnp.sum(prob * d_prob, axis=-1, keepdims=True))
        d_score = (d_score * HEAD ** (-0.5)).astype(BF16)
        d_query = dot(d_score, keyval[0]).astype(BF16)
        dpair[0] += dot(d_score, query[head], TN)
        dpair[1] += dot(prob.astype(BF16), d_head, TN)
        dquery_h[head] = d_query
        return total + d_query.astype(F32) * query[head].astype(F32)

    total = lax.fori_loop(0, heads, head_back, jnp.zeros((seq, HEAD), F32))
    for head in range(heads):
        flat[:, head * HEAD : (head + 1) * HEAD] = dquery_h[head]
    for side in range(2):
        d_low = dpair[side].astype(BF16)
        dpair_low[:, side * HEAD : (side + 1) * HEAD] = d_low
        total = total + d_low.astype(F32) * keyval[side].astype(F32)
    row_sums[t] = jnp.sum(total.T, axis=0, keepdims=True)
    for step in range(1, tensors):
        launch(
            row_sums.at[t],
            row_sums.at[t],
            row_send.at[step],
            row_recv.at[step],
            s,
            lax.rem(t + step, tensors),
        )

    def back_term(block):
        return dot(flat[...], wq[block], NT) + dot(dpair_low[...], wkv[block], NT)

    reduce_start(0, back_term)

    pass_far(FRESH)
    gathered(FRESH)
    project(FRESH)
    reduce_middle(0)

    def head_forward(head, carry):
        dquery_h[head] = dot(probability(head).astype(BF16), keyval[1]).astype(BF16)
        return carry

    lax.fori_loop(0, heads, head_forward, 0)
    for head in range(heads):
        flat[:, head * HEAD : (head + 1) * HEAD] = dquery_h[head]

    def forward_term(block):
        return dot(flat[...], wo[block])

    reduce_start(1, forward_term)

    summed = own[0] + reduce_end(0)
    for step in range(1, tensors):
        here = row_sums.at[lax.rem(t + tensors - step, tensors)]
        arrived(here, row_send.at[step], row_recv.at[step])
    row = row_sums[0]
    for block in range(1, tensors):
        row = row + row_sums[block]
    column = jnp.broadcast_to(row, (128, seq)).T[:, :1]
    inv = inv_ref[:, :1]
    result[0] = (
        full[GRAD, t].astype(F32)
        + inv * (summed * gains[t])
        - full[STASH, t].astype(F32) * (inv * inv * column / features)
    ).astype(BF16)
    grad_copy = pltpu.make_async_copy(result.at[0], input_grad.at[0], local_sem.at[2])
    grad_copy.start()
    reduce_middle(1)

    @pl.when(goes_away)
    def _():
        evict_copy.wait()

    @pl.when(jnp.logical_not(goes_away))
    def _():
        keep_copy.wait()

    grad_copy.wait()
    for copy in pending[:-2]:
        copy.wait_send()
    own[1] = full[FRESH, t].astype(F32) + own[1]
    result[1] = (own[1] + reduce_end(1)).astype(BF16)
    out_copy = pltpu.make_async_copy(result.at[1], section_out.at[0], local_sem.at[3])
    out_copy.start()
    for copy in pending[-2:]:
        copy.wait_send()
    out_copy.wait()


def hand_over(*refs):
    sources, targets = refs[:3], refs[3:6]
    staged, sems = refs[6:]
    inward = [
        pltpu.make_async_copy(sources[at], staged.at[at], sems.at[0, at]) for at in range(3)
    ]
    outward = [
        pltpu.make_async_copy(staged.at[at], targets[at], sems.at[1, at]) for at in range(3)
    ]
    for copy in inward:
        copy.start()
    for came, goes in zip(inward, outward):
        came.wait()
        goes.start()
    for copy in outward:
        copy.wait()


def local(
    embedded, outbox, loss_grad, grad_outbox, stash_held, norm_gain, w_query, w_keyval, w_out
):
    tensors = lax.axis_size("tensor")
    chips = tensors // 2
    _, seq, width = outbox.shape
    half = seq // 2
    heads = width // HEAD
    shard = jax.ShapeDtypeStruct(outbox.shape, BF16)
    dma = pltpu.SemaphoreType.DMA
    anywhere = pl.BlockSpec(memory_space=pl.ANY)
    parts = pl.pallas_call(
        kernel,
        out_shape=(shard, shard, shard),
        in_specs=[anywhere] * 9,
        out_specs=(anywhere, anywhere, anywhere),
        scratch_shapes=[
            pltpu.VMEM((3, tensors, seq, width), BF16),
            pltpu.VMEM((1, width), BF16),
            pltpu.VMEM((tensors, 1, width), F32),
            pltpu.VMEM((tensors, width, width), BF16),
            pltpu.VMEM((tensors, width, 2 * HEAD), BF16),
            pltpu.VMEM((tensors, width, width), BF16),
            pltpu.VMEM((seq, width), F32),
            pltpu.VMEM((seq, 2 * HEAD), F32),
            pltpu.VMEM((seq, width), F32),
            pltpu.VMEM((seq, 128), F32),
            pltpu.VMEM((heads, seq, HEAD), BF16),
            pltpu.VMEM((2, seq, HEAD), BF16),
            pltpu.VMEM((heads, seq, HEAD), BF16),
            pltpu.VMEM((seq, width), BF16),
            pltpu.VMEM((2, seq, HEAD), F32),
            pltpu.VMEM((seq, 2 * HEAD), BF16),
            pltpu.VMEM((tensors, 1, seq), F32),
            pltpu.VMEM((2, chips, seq, width), BF16),
            pltpu.VMEM((2, chips, seq, width), BF16),
            pltpu.VMEM((2, chips, seq, width), BF16),
            pltpu.VMEM((2, seq, width), F32),
            pltpu.VMEM((2, 2, half, width), BF16),
            pltpu.VMEM((2, 2, seq, width), BF16),
            pltpu.VMEM((2, seq, width), BF16),
            pltpu.VMEM((seq, width), BF16),
            pltpu.VMEM((heads, seq, seq), F32),
            dma((2 + tensors,)),
            dma((4,)),
            dma((tensors,)),
            dma((tensors,)),
            dma((tensors,)),
            dma((tensors,)),
            dma((3, 2, PARTS)),
            dma((3, 2, PARTS)),
            dma((3, 2, PARTS)),
            dma((3, 2, PARTS)),
            dma((3, 4, PARTS)),
            dma((3, 4, PARTS)),
            dma,
            dma,
            dma((2, chips)),
            dma((2, chips)),
            dma((2, 6)),
            dma((2, 6)),
        ],
        compiler_params=pltpu.CompilerParams(
            collective_id=0, has_side_effects=True, vmem_limit_bytes=56 * 1024 * 1024
        ),
    )(
        embedded,
        outbox,
        loss_grad,
        grad_outbox,
        stash_held,
        norm_gain,
        w_query.reshape(tensors, width, width),
        w_keyval.reshape(tensors, width, 2 * HEAD),
        w_out[0],
    )
    return pl.pallas_call(
        hand_over,
        out_shape=(shard, shard, shard),
        in_specs=[anywhere] * 3,
        out_specs=(anywhere, anywhere, anywhere),
        scratch_shapes=[pltpu.VMEM((3,) + outbox.shape, BF16), dma((2, 3))],
    )(*parts)


def solution(mesh):
    return jax.shard_map(
        local,
        mesh=mesh,
        in_specs=(
            P(None, "tensor"),
            P("section", None, "tensor"),
            P(None, "tensor"),
            P("section", None, "tensor"),
            P("section", None, "tensor"),
            P("section", "tensor"),
            P("section", None, "tensor"),
            P("section", None, "tensor"),
            P("section", "tensor", None),
        ),
        out_specs=(
            P("section", None, "tensor"),
            P("section", None, "tensor"),
            P("section", None, "tensor"),
        ),
        check_vma=False,
    )
```

```python
import jax
import jax.numpy as jnp
from jax import lax
from jax.experimental import pallas as pl
from jax.experimental.pallas import tpu as pltpu
from jax.sharding import PartitionSpec as P

HEAD = 128
EPS = 1e-05
F32 = jnp.float32
BF16 = jnp.bfloat16
NT = (((1,), (1,)), ((), ()))
TN = (((0,), (0,)), ((), ()))
STASH, GRAD, FRESH = 0, 1, 2
PARTS = 4


def dot(a, b, dims=(((1,), (0,)), ((), ()))):
    return lax.dot_general(a, b, dims, preferred_element_type=F32)


def kernel(
    embedded,
    outbox,
    loss_grad,
    grad_outbox,
    stash,
    gain,
    w_query,
    w_keyval,
    w_out,
    section_out,
    evicted,
    input_grad,
    full,
    gain_raw,
    gains,
    wq,
    wkv,
    wo,
    acc_q,
    acc_kv,
    acc_g,
    inv_ref,
    query,
    keyval,
    dquery_h,
    flat,
    dpair,
    dpair_low,
    row_sums,
    sib_out,
    sib_in,
    sums,
    own,
    ring_in,
    last_in,
    result,
    staged,
    probs,
    weight_sem,
    local_sem,
    gain_send,
    gain_recv,
    row_send,
    row_recv,
    near_send,
    near_recv,
    far_send,
    far_recv,
    sib_send,
    sib_recv,
    evict_send,
    evict_recv,
    rs_sib_send,
    rs_sib_recv,
    rs_send,
    rs_recv,
):
    sections = lax.axis_size("section")
    tensors = lax.axis_size("tensor")
    chips = tensors // 2
    s = lax.axis_index("section")
    t = lax.axis_index("tensor")
    seq, width = outbox.shape[1], outbox.shape[2]
    half = seq // 2
    features = width * tensors
    heads = width // HEAD
    halves = [pl.ds(0, half), pl.ds(half, half)]
    quarter = seq // PARTS
    quarters = [pl.ds(part * quarter, quarter) for part in range(PARTS)]
    parity = lax.rem(s, 2)
    chip = t // 2
    core = lax.rem(t, 2)

    def member(chip_index, core_index):
        return 2 * lax.rem(chip_index, chips) + core_index

    above = member(chip + parity, core)
    below = member(chip + parity + chips - 1, core)
    up = member(chip + 1, core)
    down = member(chip + chips - 1, core)
    sibling = member(chip, 1 - core)
    targets = [
        sections - 1 - s,
        lax.rem(s + sections - 1, sections),
        lax.rem(s + 1, sections),
    ]
    mirror = sections - 2 - s
    goes_away = (s != sections - 1) & (mirror != s)
    stays = mirror == s
    final = s == sections - 1

    pending = []

    def remote(src, dst, send, recv, section, tensor):
        return pltpu.make_async_remote_copy(
            src_ref=src,
            dst_ref=dst,
            send_sem=send,
            recv_sem=recv,
            device_id=(section, tensor),
            device_id_type=pl.DeviceIdType.MESH,
        )

    def launch(*args):
        copy = remote(*args)
        copy.start()
        pending.append(copy)

    def arrived(ref, send, recv):
        remote(ref, ref, send, recv, s, sibling).wait_recv()

    barrier = pltpu.get_barrier_semaphore()
    peers = [(s, lax.rem(t + step, tensors)) for step in range(1, tensors)]
    peers += [(section, tensor) for section in targets for tensor in (above, below)]
    for peer in peers:
        pl.semaphore_signal(
            barrier, inc=1, device_id=peer, device_id_type=pl.DeviceIdType.MESH
        )

    @pl.when(goes_away)
    def _():
        pl.semaphore_signal(
            barrier, inc=1, device_id=(mirror, t), device_id_type=pl.DeviceIdType.MESH
        )

    @pl.when(goes_away)
    def _():
        pl.semaphore_wait(barrier, len(peers) + 1)

    @pl.when(jnp.logical_not(goes_away))
    def _():
        pl.semaphore_wait(barrier, len(peers))

    def near(which, src, parts):
        return [
            remote(
                src.at[quarters[part]],
                full.at[which, t, quarters[part]],
                near_send.at[which, side, part],
                near_recv.at[which, side, part],
                targets[which],
                tensor,
            )
            for part in parts
            for side, tensor in enumerate((above, below))
        ]

    def near_start(which, src):
        for copy in near(which, src, range(PARTS)):
            copy.start()

    def fresh_start():
        @pl.when(final)
        def _():
            near_start(FRESH, embedded)

        @pl.when(jnp.logical_not(final))
        def _():
            near_start(FRESH, outbox.at[0])

    def grad_start():
        @pl.when(s == 0)
        def _():
            near_start(GRAD, loss_grad)

        @pl.when(s != 0)
        def _():
            near_start(GRAD, grad_outbox.at[0])

    low = lax.rem(chip + parity + chips - 1, chips)
    high = lax.rem(chip + parity, chips)
    slots = [low, high, lax.rem(low + chips - 1, chips), lax.rem(high + 1, chips)]

    def pass_near(which, after=None, parts=range(PARTS)):
        for part in parts:
            rows = quarters[part]
            for side, ahead in enumerate((up, down)):
                here = full.at[which, 2 * slots[side] + core, rows]
                arrived(here, near_send.at[which, side, part], near_recv.at[which, side, part])
                launch(
                    here,
                    here,
                    far_send.at[which, side, part],
                    far_recv.at[which, side, part],
                    s,
                    ahead,
                )
                launch(
                    here,
                    here,
                    sib_send.at[which, side, part],
                    sib_recv.at[which, side, part],
                    s,
                    sibling,
                )
            if after is not None:
                after(part)

    def pass_far(which):
        for part, rows in enumerate(quarters):
            for side in range(2):
                here = full.at[which, 2 * slots[2 + side] + core, rows]
                arrived(here, far_send.at[which, side, part], far_recv.at[which, side, part])
                launch(
                    here,
                    here,
                    sib_send.at[which, 2 + side, part],
                    sib_recv.at[which, 2 + side, part],
                    s,
                    sibling,
                )

    def gathered(which, places=(0, 1, 2, 3)):
        for part, rows in enumerate(quarters):
            for place in places:
                here = full.at[which, 2 * slots[place] + 1 - core, rows]
                arrived(here, sib_send.at[which, place, part], sib_recv.at[which, place, part])

    def project(which):
        def squares(block, total):
            value = full[which, block].astype(F32)
            value = value * value
            for piece in range(width // 128):
                total = total + value[:, piece * 128 : (piece + 1) * 128]
            return total

        total = lax.fori_loop(0, tensors, squares, jnp.zeros((seq, 128), F32))
        inv = lax.rsqrt(jnp.sum(total, axis=-1, keepdims=True) / features + EPS)
        acc_q[...] = jnp.zeros_like(acc_q)
        acc_kv[...] = jnp.zeros_like(acc_kv)

        def step(block, carry):
            normed = (full[which, block].astype(F32) * inv * gains[block]).astype(BF16)
            acc_q[...] += dot(normed, wq[block])
            acc_kv[...] += dot(normed, wkv[block])
            return carry

        lax.fori_loop(0, tensors, step, 0)
        for head in range(heads):
            query[head] = acc_q[:, head * HEAD : (head + 1) * HEAD].astype(BF16)
        for side in range(2):
            keyval[side] = acc_kv[:, side * HEAD : (side + 1) * HEAD].astype(BF16)
        return inv

    def probability(head):
        scores = dot(query[head], keyval[0], NT) * HEAD ** (-0.5)
        rows = lax.broadcasted_iota(jnp.int32, (seq, seq), 0)
        cols = lax.broadcasted_iota(jnp.int32, (seq, seq), 1)
        scores = jnp.where(rows >= cols, scores, -1e30)
        top = jnp.max(scores, axis=-1, keepdims=True)
        raised = jnp.exp(scores - top)
        return raised / jnp.sum(raised, axis=-1, keepdims=True)

    def chip_at(turn):
        return lax.rem(chip + 2 + chips - turn, chips)

    def reduce_start(which, term):
        def to_sibling(turn):
            return remote(
                sib_out.at[which, turn],
                sib_in.at[which, turn],
                rs_sib_send.at[which, turn],
                rs_sib_recv.at[which, turn],
                s,
                sibling,
            )

        opening = [
            (0, 0, 0, ring_in.at[which, 0], up),
            (0, 1, 1, ring_in.at[which, 1], down),
            (1, 1, 2, last_in.at[which, 0, halves[1]], up),
            (3, 0, 3, last_in.at[which, 1, halves[0]], down),
        ]

        def sends(turn):
            return [
                remote(
                    sums.at[which, at, halves[part]],
                    dst,
                    rs_send.at[which, sem],
                    rs_recv.at[which, sem],
                    s,
                    tensor,
                )
                for at, part, sem, dst, tensor in opening
                if at == turn
            ]

        def step(stage, carry):
            @pl.when(stage < chips)
            def _():
                sib_out[which, stage] = term(2 * chip_at(stage) + 1 - core).astype(BF16)
                to_sibling(stage).start()

            @pl.when(stage > 0)
            def _():
                turn = stage - 1
                mine = term(2 * chip_at(turn) + core)
                arrived(
                    sib_in.at[which, turn],
                    rs_sib_send.at[which, turn],
                    rs_sib_recv.at[which, turn],
                )
                total = mine + sib_in[which, turn].astype(F32)
                sums[which, turn] = total.astype(BF16)

                @pl.when(turn == 2)
                def _():
                    own[which] = total

                for at in (0, 1, 3) if which == 0 else (0,):

                    @pl.when(turn == at)
                    def _():
                        for copy in sends(at):
                            copy.start()

            return carry

        lax.fori_loop(0, chips + 1, step, 0)
        pending.extend(to_sibling(turn) for turn in range(chips))
        if which == 0:
            for at in (0, 1, 3):
                pending.extend(sends(at))
        return sends(0), sends(1) + sends(3)

    def reduce_middle(which):
        for side, (turn, part, ahead) in enumerate(((1, 0, up), (3, 1, down))):
            rows = halves[part]
            arrived(ring_in.at[which, side], rs_send.at[which, side], rs_recv.at[which, side])
            sums[which, turn, rows] = (
                sums[which, turn, rows].astype(F32) + ring_in[which, side].astype(F32)
            ).astype(BF16)
            launch(
                sums.at[which, turn, rows],
                last_in.at[which, side, rows],
                rs_send.at[which, 4 + side],
                rs_recv.at[which, 4 + side],
                s,
                ahead,
            )

    def reduce_end(which):
        arrived(last_in.at[which, 0, halves[1]], rs_send.at[which, 2], rs_recv.at[which, 2])
        arrived(last_in.at[which, 1, halves[0]], rs_send.at[which, 3], rs_recv.at[which, 3])
        arrived(last_in.at[which, 0, halves[0]], rs_send.at[which, 4], rs_recv.at[which, 4])
        arrived(last_in.at[which, 1, halves[1]], rs_send.at[which, 5], rs_recv.at[which, 5])
        return last_in[which, 0].astype(F32) + last_in[which, 1].astype(F32)

    for copy in near(STASH, stash.at[0], (0, 1)):
        copy.start()

    @pl.when(parity == 0)
    def _():
        fresh_start()

    @pl.when(parity == 1)
    def _():
        grad_start()

    gain_copy = pltpu.make_async_copy(gain, gain_raw, local_sem.at[0])
    gain_copy.start()
    weights = [
        pltpu.make_async_copy(w_query, wq, weight_sem.at[0]),
        pltpu.make_async_copy(w_keyval, wkv, weight_sem.at[1]),
    ]
    for block in range(tensors):
        weights.append(
            pltpu.make_async_copy(
                w_out.at[:, pl.ds(block * width, width)], wo.at[block], weight_sem.at[2 + block]
            )
        )
    for copy in weights:
        copy.start()
    gain_copy.wait()

    @pl.when(final)
    def _():
        pltpu.make_async_copy(embedded, staged, local_sem.at[1]).start()

    @pl.when(jnp.logical_not(final))
    def _():
        pltpu.make_async_copy(outbox.at[0], staged, local_sem.at[1]).start()

    gains[t] = gain_raw[...].astype(F32)

    for step in range(1, tensors):
        launch(
            gains.at[t],
            gains.at[t],
            gain_send.at[step],
            gain_recv.at[step],
            s,
            lax.rem(t + step, tensors),
        )

    def more_stash(part):
        for copy in near(STASH, stash.at[0], (part,)):
            copy.wait_send()
        if part + 2 < PARTS:
            for copy in near(STASH, stash.at[0], (part + 2,)):
                copy.start()

    pass_near(STASH, more_stash)

    @pl.when(parity == 1)
    def _():
        fresh_start()

    @pl.when(parity == 0)
    def _():
        grad_start()

    pending.extend(near(GRAD, grad_outbox.at[0], range(PARTS)))
    pending.extend(near(FRESH, outbox.at[0], range(PARTS)))
    pass_far(STASH)
    pass_near(GRAD)
    for step in range(1, tensors):
        here = gains.at[lax.rem(t + tensors - step, tensors)]
        arrived(here, gain_send.at[step], gain_recv.at[step])
    for copy in weights:
        copy.wait()
    gathered(STASH)
    pltpu.make_async_copy(outbox.at[0], staged, local_sem.at[1]).wait()
    evict_copy = remote(staged, evicted.at[0], evict_send, evict_recv, mirror, t)
    keep_copy = pltpu.make_async_copy(staged, evicted.at[0], local_sem.at[1])

    @pl.when(goes_away)
    def _():
        evict_copy.start()

    @pl.when(jnp.logical_not(goes_away))
    def _():
        keep_copy.start()

    inv_back = project(STASH)
    inv_ref[...] = jnp.broadcast_to(inv_back, inv_ref.shape)

    def keep_probability(head, carry):
        probs[head] = probability(head)
        return carry

    lax.fori_loop(0, heads, keep_probability, 0)
    acc_g[...] = jnp.zeros_like(acc_g)

    def pull_back(places):
        def step(at, carry):
            block = 2 * slots[places[0]] + at
            other = 2 * slots[places[1]] + at
            acc_g[...] += dot(full[GRAD, block], wo[block], NT) + dot(
                full[GRAD, other], wo[other], NT
            )
            return carry

        gathered(GRAD, places)
        lax.fori_loop(0, 2, step, 0)

    pull_back((0, 1))
    pass_near(FRESH, parts=(0, 1))
    pass_far(GRAD)
    pass_near(FRESH, parts=(2, 3))
    pull_back((2, 3))
    for head in range(heads):
        dquery_h[head] = acc_g[:, head * HEAD : (head + 1) * HEAD].astype(BF16)
    dpair[...] = jnp.zeros_like(dpair)

    def head_back(head, total):
        prob = probs[head]
        d_head = dquery_h[head]
        d_prob = dot(d_head, keyval[1], NT)
        d_score = prob * (d_prob - jnp.sum(prob * d_prob, axis=-1, keepdims=True))
        d_score = (d_score * HEAD ** (-0.5)).astype(BF16)
        d_query = dot(d_score, keyval[0]).astype(BF16)
        dpair[0] += dot(d_score, query[head], TN)
        dpair[1] += dot(prob.astype(BF16), d_head, TN)
        dquery_h[head] = d_query
        return total + d_query.astype(F32) * query[head].astype(F32)

    total = lax.fori_loop(0, heads, head_back, jnp.zeros((seq, HEAD), F32))
    for head in range(heads):
        flat[:, head * HEAD : (head + 1) * HEAD] = dquery_h[head]
    for side in range(2):
        d_low = dpair[side].astype(BF16)
        dpair_low[:, side * HEAD : (side + 1) * HEAD] = d_low
        total = total + d_low.astype(F32) * keyval[side].astype(F32)
    row_sums[t] = jnp.sum(total.T, axis=0, keepdims=True)
    for step in range(1, tensors):
        launch(
            row_sums.at[t],
            row_sums.at[t],
            row_send.at[step],
            row_recv.at[step],
            s,
            lax.rem(t + step, tensors),
        )

    def back_term(block):
        return dot(flat[...], wq[block], NT) + dot(dpair_low[...], wkv[block], NT)

    reduce_start(0, back_term)

    pass_far(FRESH)
    gathered(FRESH)
    project(FRESH)
    reduce_middle(0)

    def head_forward(head, carry):
        dquery_h[head] = dot(probability(head).astype(BF16), keyval[1]).astype(BF16)
        return carry

    lax.fori_loop(0, heads, head_forward, 0)
    for head in range(heads):
        flat[:, head * HEAD : (head + 1) * HEAD] = dquery_h[head]

    def forward_term(block):
        return dot(flat[...], wo[block])

    opposite, nearest = reduce_start(1, forward_term)

    summed = own[0] + reduce_end(0)
    for step in range(1, tensors):
        here = row_sums.at[lax.rem(t + tensors - step, tensors)]
        arrived(here, row_send.at[step], row_recv.at[step])
    row = row_sums[0]
    for block in range(1, tensors):
        row = row + row_sums[block]
    column = jnp.broadcast_to(row, (128, seq)).T[:, :1]
    inv = inv_ref[:, :1]
    result[0] = (
        full[GRAD, t].astype(F32)
        + inv * (summed * gains[t])
        - full[STASH, t].astype(F32) * (inv * inv * column / features)
    ).astype(BF16)
    grad_copy = pltpu.make_async_copy(result.at[0], input_grad.at[0], local_sem.at[2])
    grad_copy.start()
    for copy in opposite:
        copy.wait_send()
    for copy in nearest:
        copy.start()
    pending.extend(nearest)
    reduce_middle(1)

    @pl.when(goes_away)
    def _():
        evict_copy.wait()

    @pl.when(jnp.logical_not(goes_away))
    def _():
        keep_copy.wait()

    grad_copy.wait()
    for copy in pending[:-2]:
        copy.wait_send()
    own[1] = full[FRESH, t].astype(F32) + own[1]
    result[1] = (own[1] + reduce_end(1)).astype(BF16)
    out_copy = pltpu.make_async_copy(result.at[1], section_out.at[0], local_sem.at[3])
    out_copy.start()
    for copy in pending[-2:]:
        copy.wait_send()
    out_copy.wait()


def hand_over(*refs):
    sources, targets = refs[:3], refs[3:6]
    staged, sems = refs[6:]
    inward = [
        pltpu.make_async_copy(sources[at], staged.at[at], sems.at[0, at]) for at in range(3)
    ]
    outward = [
        pltpu.make_async_copy(staged.at[at], targets[at], sems.at[1, at]) for at in range(3)
    ]
    for copy in inward:
        copy.start()
    for came, goes in zip(inward, outward):
        came.wait()
        goes.start()
    for copy in outward:
        copy.wait()


def local(
    embedded, outbox, loss_grad, grad_outbox, stash_held, norm_gain, w_query, w_keyval, w_out
):
    tensors = lax.axis_size("tensor")
    chips = tensors // 2
    _, seq, width = outbox.shape
    half = seq // 2
    heads = width // HEAD
    shard = jax.ShapeDtypeStruct(outbox.shape, BF16)
    dma = pltpu.SemaphoreType.DMA
    anywhere = pl.BlockSpec(memory_space=pl.ANY)
    parts = pl.pallas_call(
        kernel,
        out_shape=(shard, shard, shard),
        in_specs=[anywhere] * 9,
        out_specs=(anywhere, anywhere, anywhere),
        scratch_shapes=[
            pltpu.VMEM((3, tensors, seq, width), BF16),
            pltpu.VMEM((1, width), BF16),
            pltpu.VMEM((tensors, 1, width), F32),
            pltpu.VMEM((tensors, width, width), BF16),
            pltpu.VMEM((tensors, width, 2 * HEAD), BF16),
            pltpu.VMEM((tensors, width, width), BF16),
            pltpu.VMEM((seq, width), F32),
            pltpu.VMEM((seq, 2 * HEAD), F32),
            pltpu.VMEM((seq, width), F32),
            pltpu.VMEM((seq, 128), F32),
            pltpu.VMEM((heads, seq, HEAD), BF16),
            pltpu.VMEM((2, seq, HEAD), BF16),
            pltpu.VMEM((heads, seq, HEAD), BF16),
            pltpu.VMEM((seq, width), BF16),
            pltpu.VMEM((2, seq, HEAD), F32),
            pltpu.VMEM((seq, 2 * HEAD), BF16),
            pltpu.VMEM((tensors, 1, seq), F32),
            pltpu.VMEM((2, chips, seq, width), BF16),
            pltpu.VMEM((2, chips, seq, width), BF16),
            pltpu.VMEM((2, chips, seq, width), BF16),
            pltpu.VMEM((2, seq, width), F32),
            pltpu.VMEM((2, 2, half, width), BF16),
            pltpu.VMEM((2, 2, seq, width), BF16),
            pltpu.VMEM((2, seq, width), BF16),
            pltpu.VMEM((seq, width), BF16),
            pltpu.VMEM((heads, seq, seq), F32),
            dma((2 + tensors,)),
            dma((4,)),
            dma((tensors,)),
            dma((tensors,)),
            dma((tensors,)),
            dma((tensors,)),
            dma((3, 2, PARTS)),
            dma((3, 2, PARTS)),
            dma((3, 2, PARTS)),
            dma((3, 2, PARTS)),
            dma((3, 4, PARTS)),
            dma((3, 4, PARTS)),
            dma,
            dma,
            dma((2, chips)),
            dma((2, chips)),
            dma((2, 6)),
            dma((2, 6)),
        ],
        compiler_params=pltpu.CompilerParams(
            collective_id=0, has_side_effects=True, vmem_limit_bytes=56 * 1024 * 1024
        ),
    )(
        embedded,
        outbox,
        loss_grad,
        grad_outbox,
        stash_held,
        norm_gain,
        w_query.reshape(tensors, width, width),
        w_keyval.reshape(tensors, width, 2 * HEAD),
        w_out[0],
    )
    return pl.pallas_call(
        hand_over,
        out_shape=(shard, shard, shard),
        in_specs=[anywhere] * 3,
        out_specs=(anywhere, anywhere, anywhere),
        scratch_shapes=[pltpu.VMEM((3,) + outbox.shape, BF16), dma((2, 3))],
    )(*parts)


def solution(mesh):
    return jax.shard_map(
        local,
        mesh=mesh,
        in_specs=(
            P(None, "tensor"),
            P("section", None, "tensor"),
            P(None, "tensor"),
            P("section", None, "tensor"),
            P("section", None, "tensor"),
            P("section", "tensor"),
            P("section", None, "tensor"),
            P("section", None, "tensor"),
            P("section", "tensor", None),
        ),
        out_specs=(
            P("section", None, "tensor"),
            P("section", None, "tensor"),
            P("section", None, "tensor"),
        ),
        check_vma=False,
    )
```
